512 devices in a mesh: wide: 64 (over x, z), narrow: 8 (over y, core).
Axes of the slice: x: 4, y: 4, z: 16, core: 2. Of those that a mesh axis runs over, the one named last changes fastest.
Arguments:
- residual: bfloat16 [256, 16384], P('narrow', 'wide'), may hold values from -54 to 54
- norm_gain: bfloat16 [16384], P('wide'), may hold values from 0.5 to 1.5
- w_query: bfloat16 [16384, 16384], P('wide', 'narrow'), may hold values from -0.046875 to 0.046875
- w_keyval: bfloat16 [16384, 2, 1024], P('wide', None, 'narrow'), may hold values from -0.046875 to 0.046875
- w_out: bfloat16 [16384, 16384], P('narrow', 'wide'), may hold values from -0.375 to 0.375
- cache_rows: bfloat16 [256, 768, 2, 1024], P('wide', None, None, 'narrow'), may hold values from -106 to 106, as said below
- lengths: int32 [256], replicated, may hold values from 1 to 768, 49152 in all
- assignment: int32 [256], replicated, may hold values from 0 to 255, each once
Outputs:
- layer_out: bfloat16 [256, 16384], P('narrow', 'wide')
The draws below stay inside these ranges and needn't reach their ends.
Inputs may be any that keep to these rules, and one draw needn't show every extreme that they name: `lengths`: largest entry reaches 768. `assignment`: each row named once. `cache_rows`: entries at positions at or beyond a row's length are not read.
All inputs are finite; a program needn't handle non-finite values.
Results may differ from the reference program's by a relative error of at most 0.012.
The reference program's roundings to bfloat16 on the way (of `normed`, `queries`, `probs` and `attended`) count: a program that leaves them out, or rounds other values in their place, can miss the bound.
Values may be sent and summed in bfloat16 or wider, within the bound.
A program may use at most 64 MiB of HBM per device.

```python
import math
import jax
import jax.numpy as jnp
import numpy as np
from jax import lax

D = 16384
H = 128
KVH = 8
HD = 128
MEAN_LEN = 192
ROWS = 256
MOST = 768


def draw_residual(key, part):
    first, second, third = jax.random.split(jax.random.fold_in(key, 11), 3)
    jitter = jnp.clip(jax.random.normal(first, (ROWS, D), jnp.float32), -4.0, 4.0)
    rising = 3.0 ** (jnp.arange(D, dtype=jnp.float32) / D - 0.5)
    column_scale = jnp.exp(jax.random.uniform(second, (D,), jnp.float32, -0.8, 0.8)) * rising
    row_scale = jnp.exp(jax.random.uniform(third, (ROWS, 1), jnp.float32, -0.693, 0.693))
    return (jitter * column_scale[None, :] * row_scale).astype(jnp.bfloat16)


def draw_cache_rows(key, part):
    first = jax.random.fold_in(jax.random.fold_in(key, 23), 0)
    stored = jnp.clip(jax.random.normal(first, (ROWS, MOST, 2, KVH * HD), jnp.float32), -5.0, 5.0)
    return stored.astype(jnp.bfloat16)


def level_of(key, shape, pieces, least, top_value):
    level, own = 1.0, jax.random.fold_in(key, 6)
    for dim, parts in pieces:
        steps = jnp.exp(jax.random.uniform(jax.random.fold_in(own, dim), (parts,), jnp.float32, least / len(pieces), top_value / len(pieces)))
        level = level * jnp.repeat(steps, shape[dim] // parts).reshape([-1 if axis == dim else 1 for axis in range(len(shape))])
    return level


def profile(count, total, most, slope):
    loads = [(1 << 20) // math.isqrt(rank ** slope) + 1 for rank in range(2, count + 1)]
    rest, holding = total - most - (count - 1), [1] * (count - 1)
    while rest > 0:
        candidates = [i for i in range(count - 1) if holding[i] < most]
        whole, budget = sum([loads[i] for i in candidates]), rest
        for i in candidates:
            more = min(most - holding[i], max(1, budget * loads[i] // whole), rest)
            holding[i] = holding[i] + more
            rest = rest - more
    return np.array([most] + holding)


def ragged(rng, number_of, total, most, slope):
    if number_of == 2:
        one = jax.random.randint(rng, (), max(1, total - most), min(most, total - 1) + 1)
        return jnp.stack([one, total - one])
    sizes = jnp.asarray(profile(number_of, total, most, slope), jnp.int32)
    twos = (number_of - 1) // 2
    donor, receiver = sizes[1:1 + 2 * twos:2], sizes[2:2 + 2 * twos:2]
    margin = jnp.minimum(donor - 1, most - receiver)
    moved = jax.random.randint(jax.random.fold_in(rng, 1), (twos,), 0, 1 << 20) % (margin + 1)
    sizes = sizes.at[1:1 + 2 * twos:2].set(donor - moved).at[2:2 + 2 * twos:2].set(receiver + moved)
    return sizes[jax.random.permutation(jax.random.fold_in(rng, 2), number_of)]


def gaussian(stream_key, dims, spread, reach, shards=(), kind=jnp.bfloat16):
    result = jax.random.normal(stream_key, dims, jnp.float32) * spread
    if len(shards) > 0:
        result = level_of(stream_key, dims, shards, -0.22, 0.18) * result
    return jnp.clip(result, min=-reach, max=reach).astype(kind)


def setup_inputs(seed: int = 0) -> dict:
    streams_of = jax.random.split(jax.random.key(seed), 9)
    residual = draw_residual(jax.random.fold_in(streams_of[8], 71), 0)
    norm_gain = jnp.clip(1.0 + 0.1 * jax.random.normal(streams_of[1], (D,), jnp.float32), 0.5, 1.5).astype(jnp.bfloat16)
    w_query = gaussian(streams_of[2], (D, H * HD), D ** -0.5, 0.046875, ((0, 64), (1, 8)))
    w_keyval = gaussian(streams_of[3], (D, 2, KVH * HD), D ** -0.5, 0.046875, ((0, 64), (2, 8)))
    w_out = gaussian(streams_of[4], (H * HD, D), (H * HD // 64) ** -0.5, 0.375, ((0, 8), (1, 64)))
    cache_rows = draw_cache_rows(jax.random.fold_in(streams_of[8], 71), 0)
    lengths = ragged(streams_of[6], ROWS, ROWS * MEAN_LEN, MOST, 2).astype(jnp.int32)
    assignment = jax.random.permutation(streams_of[7], ROWS).astype(jnp.int32)
    return {"residual": residual, "norm_gain": norm_gain, "w_query": w_query, "w_keyval": w_keyval, "w_out": w_out, "cache_rows": cache_rows, "lengths": lengths, "assignment": assignment}


def rotate(values, positions):
    half_dim = values.shape[-1] // 2
    freqs = 500000.0 ** (-(jnp.arange(half_dim, dtype=jnp.float32) * 2.0 / values.shape[-1]))
    angles = positions[..., None] * freqs
    cosine = jnp.cos(angles)
    sine = jnp.sin(angles)
    first_half = values[..., :half_dim]
    second_half = values[..., half_dim:]
    return jnp.concatenate([first_half * cosine - second_half * sine, second_half * cosine + first_half * sine], axis=-1)

def reference(residual, norm_gain, w_query, w_keyval, w_out, cache_rows, lengths, assignment):
    inputs = residual.astype(jnp.float32)
    inverse_rms = lax.rsqrt(lax.optimization_barrier(jnp.mean(inputs * inputs, axis=1, keepdims=True)) + 1e-05)
    normed = (inputs * inverse_rms * norm_gain.astype(jnp.float32)).astype(jnp.bfloat16)
    query_raw = jnp.dot(normed, w_query, preferred_element_type=jnp.float32)
    keyval_raw = jnp.dot(normed, w_keyval.reshape(D, 2 * KVH * HD), preferred_element_type=jnp.float32)
    keyval_raw = keyval_raw.reshape(ROWS, 2, KVH, HD)
    positions = lengths.astype(jnp.float32)[:, None]
    queries = rotate(query_raw.reshape(ROWS, H, HD), positions).astype(jnp.bfloat16)
    keys_new = rotate(keyval_raw[:, 0], positions).astype(jnp.bfloat16)
    values_new = keyval_raw[:, 1].astype(jnp.bfloat16)
    slot_of = jnp.zeros((ROWS,), jnp.int32).at[assignment].set(jnp.arange(ROWS, dtype=jnp.int32))
    group_size = H // KVH
    scale = 1.0 / math.sqrt(HD)

    def attend_row(row_id):
        slot_id = slot_of[row_id]
        stored = lax.dynamic_index_in_dim(cache_rows, slot_id, 0, keepdims=False).astype(jnp.float32)
        keys = stored[:, 0].reshape(MOST, KVH, HD)
        values = stored[:, 1].reshape(MOST, KVH, HD)
        query = queries[row_id].astype(jnp.float32).reshape(KVH, group_size, HD)
        scores = jnp.einsum('kgd,jkd->kgj', query, keys) * scale
        live_mask = jnp.arange(MOST, dtype=jnp.int32) < lengths[row_id]
        scores = jnp.where(live_mask[None, None, :], scores, -jnp.inf)
        own_score = jnp.einsum('kgd,kd->kg', query, keys_new[row_id].astype(jnp.float32)) * scale
        maxima = jnp.maximum(lax.optimization_barrier(jnp.max(scores, axis=-1)), own_score)
        weights = jnp.exp(scores - maxima[..., None])
        own_weight = jnp.exp(own_score - maxima)
        totals = lax.optimization_barrier(jnp.sum(weights, axis=-1)) + own_weight
        probs = lax.optimization_barrier((weights / totals[..., None]).astype(jnp.bfloat16)).astype(jnp.float32)
        own_prob = lax.optimization_barrier((own_weight / totals).astype(jnp.bfloat16)).astype(jnp.float32)
        attended = jnp.einsum('kgj,jkd->kgd', probs, values)
        attended = attended + own_prob[..., None] * values_new[row_id].astype(jnp.float32)[:, None, :]
        return attended.reshape(H * HD).astype(jnp.bfloat16)
    attended_rows = lax.map(attend_row, jnp.arange(ROWS, dtype=jnp.int32))
    update = jnp.dot(attended_rows, w_out, preferred_element_type=jnp.float32)
    return (inputs + update).astype(jnp.bfloat16)
```

```python
import functools
import math

import jax
import jax.numpy as jnp
import numpy as np
from jax import lax
from jax.experimental import pallas as pl
from jax.experimental.pallas import tpu as pltpu
from jax.sharding import Mesh
from jax.sharding import PartitionSpec as P

HD = 128
MESH = pl.DeviceIdType.MESH
F32 = jnp.float32
BF16 = jnp.bfloat16


def rotation_table(most):
    half = HD // 2
    exponents = -(np.arange(half, dtype=np.float32) * np.float32(2.0) / np.float32(HD))
    freqs = np.power(np.float32(500000.0), exponents).astype(np.float32)
    rows = (most + 8) // 8 * 8
    angles = (np.arange(rows, dtype=np.float32)[:, None] * freqs[None, :]).astype(np.float32)
    angles = angles.astype(np.float64)
    return np.concatenate([np.cos(angles), np.sin(angles)], axis=1).astype(np.float32)


def dot(a, b):
    return lax.dot_general(a, b, (((1,), (0,)), ((), ())), preferred_element_type=F32)


def dot_t(a, b):
    return lax.dot_general(a, b, (((1,), (1,)), ((), ())), preferred_element_type=F32)


def by_distance(count):
    return sorted(range(1, count), key=lambda d: min(d, count - d))


def kernel(
    nx, nz, nn, width,
    lens, asg, res_h, gain_ref, asg_ref, wq_h, wkv_h, wo_h, cache_h, tab_h,
    out_ref,
    nres, gains, wq, wkv, kvs, kvw, wo, cache, kc, vc, tab,
    zin, nsq, pz, pr, sres, nrm, part, rbuf, lbuf, xs, xin, q_ref, ab, ag, att, nst, nin,
    loc, xr_s, xr_r, xg_s, xg_r, xw_s, xw_r, kv_s, kv_r, ng_s, ng_r,
    zs_s, zs_r, ns_s, ns_r, rr_s, rr_r, lr_s, lr_r, xe_s, xe_r,
    az_s, az_r, ax_s, ax_r, no_s, no_r,
):
    x, z, n = lax.axis_index("x"), lax.axis_index("z"), lax.axis_index("narrow")
    rows = pz.shape[0]
    rows_n = rows // nn
    slots = xs.shape[1]
    per_z = nx * slots
    qcols = wq.shape[2]
    kw = wq.shape[1]
    most = kc.shape[1]
    heads = q_ref.shape[1]
    heads_x = heads // nx
    w_own = x * nz + z

    def remote(src, dst, ss, rs, dev):
        return pltpu.make_async_remote_copy(
            src_ref=src, dst_ref=dst, send_sem=ss, recv_sem=rs, device_id=dev, device_id_type=MESH
        )

    def at_x(d):
        return lax.rem(x + d, nx)

    def at_z(d):
        return lax.rem(z + d, nz)

    def at_n(d):
        return lax.rem(n + d, nn)

    def wq_part(t):
        return wq_h.at[:, pl.ds(pl.multiple_of(t * qcols, qcols), qcols)]

    local = [
        pltpu.make_async_copy(wkv_h, wkv, loc.at[0]),
        pltpu.make_async_copy(res_h, nres.at[n, x], loc.at[1]),
        pltpu.make_async_copy(wq_part(x), wq.at[x], loc.at[2]),
        pltpu.make_async_copy(cache_h, cache, loc.at[3]),
        pltpu.make_async_copy(wo_h, wo, loc.at[4]),
        pltpu.make_async_copy(tab_h, tab, loc.at[5]),
    ]
    barrier = pltpu.get_barrier_semaphore()
    for d in reversed(by_distance(nz)):
        pl.semaphore_signal(barrier, inc=1, device_id={"z": at_z(d)}, device_id_type=MESH)
    for d in range(1, nx):
        pl.semaphore_signal(barrier, inc=1, device_id={"x": at_x(d)}, device_id_type=MESH)
    for d in range(1, nn):
        pl.semaphore_signal(barrier, inc=1, device_id={"narrow": at_n(d)}, device_id_type=MESH)
    for copy in local:
        copy.start()

    a_row = asg_ref[...]
    i_sub = lax.broadcasted_iota(jnp.int32, (rows, rows), 0)
    i_lane = lax.broadcasted_iota(jnp.int32, (rows, rows), 1)
    zz, rest = i_sub // per_z, i_sub % per_z
    slot_of = ((rest // slots) * nz + zz) * slots + rest % slots
    a_col = jnp.sum(
        jnp.where(i_lane == slot_of, a_row.astype(F32), 0.0), axis=1, keepdims=True
    ).astype(jnp.int32)
    pick = i_lane == a_col
    pz[...] = jnp.where(pick, 1.0, 0.0).astype(BF16)
    pr[...] = jnp.where(i_sub == a_row, 1.0, 0.0).astype(BF16)
    gains[x] = gain_ref[...].astype(F32)

    e_row = lax.broadcasted_iota(jnp.int32, (kw, 2 * kw), 0)
    e_col = lax.broadcasted_iota(jnp.int32, (kw, 2 * kw), 1)
    e0 = jnp.where(e_col == 2 * e_row, 1.0, 0.0).astype(BF16)
    e1 = jnp.where(e_col == 2 * e_row + 1, 1.0, 0.0).astype(BF16)
    local[0].wait()
    kvs[0] = dot(e0, wkv[...]).astype(BF16)
    kvs[1] = dot(e1, wkv[...]).astype(BF16)

    pl.semaphore_wait(barrier, (nx - 1) + (nz - 1) + (nn - 1))

    sends = []

    def send(copy):
        copy.start()
        sends.append(copy)

    for d in range(1, nx):
        dev = {"x": at_x(d)}
        send(remote(res_h, nres.at[n, x], xr_s.at[d], xr_r.at[d], dev))
        send(remote(gains.at[x], gains.at[x], xg_s.at[d], xg_r.at[d], dev))
    for d in range(1, nx):
        send(remote(wq_part(at_x(d)), wq.at[x], xw_s.at[d], xw_r.at[d], {"x": at_x(d)}))
    kv_slot = lax.rem(x, 2)
    k_copy = remote(kvs.at[0], kvw.at[kv_slot], kv_s.at[0], kv_r.at[kv_slot], {"x": x // 2})
    v_copy = remote(kvs.at[1], kvw.at[kv_slot], kv_s.at[1], kv_r.at[kv_slot], {"x": 2 + x // 2})

    @pl.when(x != 0)
    def _():
        k_copy.start()

    @pl.when(x == 0)
    def _():
        kvw[0] = kvs[0]

    @pl.when(x != nx - 1)
    def _():
        v_copy.start()

    @pl.when(x == nx - 1)
    def _():
        kvw[1] = kvs[1]

    local[1].wait()
    for d in range(1, nx):
        src = at_x(nx - d)
        remote(res_h, nres.at[n, src], xr_s.at[d], xr_r.at[d], {"x": src}).wait_recv()
    for d in range(1, nn):
        send(remote(nres.at[n], nres.at[n], ng_s.at[d], ng_r.at[d], {"narrow": at_n(d)}))

    squares = jnp.zeros((rows_n, 1), F32)
    for k in range(nx):
        block = nres[n, k].astype(F32)
        squares = squares + jnp.sum(block * block, axis=1, keepdims=True)
    r_sub = lax.broadcasted_iota(jnp.int32, (rows_n, rows), 0)
    r_lane = lax.broadcasted_iota(jnp.int32, (rows_n, rows), 1)
    zin[z] = jnp.sum(jnp.where(r_lane == r_sub + n * rows_n, squares, 0.0), axis=0, keepdims=True)
    for d in reversed(by_distance(nz)):
        send(remote(zin.at[z], zin.at[z], zs_s.at[d], zs_r.at[d], {"z": at_z(d)}))

    local[3].wait()
    step = kw
    for j in range(slots):
        for b in range(most // step):
            block = cache[pl.ds((j * most + b * step) * 2, 2 * step), :]
            kc[j, b * step : (b + 1) * step, :] = dot(e0, block).astype(BF16)
            vc[j, b * step : (b + 1) * step, :] = dot(e1, block).astype(BF16)

    for d in range(1, nn):
        src = at_n(nn - d)
        remote(nres.at[src], nres.at[src], ng_s.at[d], ng_r.at[d], {"narrow": src}).wait_recv()
    for k in range(nx):
        block = nres[:, k].reshape(rows, kw)
        sres[:, k * kw : (k + 1) * kw] = dot(pz[...], block).astype(BF16)

    for d in range(1, nz):
        src = at_z(nz - d)
        remote(zin.at[src], zin.at[src], zs_s.at[d], zs_r.at[d], {"z": src}).wait_recv()
    nsq[n] = jnp.sum(zin[...], axis=0)
    for d in range(1, nn):
        send(remote(nsq.at[n], nsq.at[n], ns_s.at[d], ns_r.at[d], {"narrow": at_n(d)}))
    for d in range(1, nn):
        src = at_n(nn - d)
        remote(nsq.at[src], nsq.at[src], ns_s.at[d], ns_r.at[d], {"narrow": src}).wait_recv()
    sums = jnp.sum(nsq[...], axis=0)
    sum_col = jnp.sum(jnp.where(pz[...].astype(F32) > 0.5, sums, 0.0), axis=1, keepdims=True)
    inverse = lax.rsqrt(sum_col / width + 1e-05)

    for d in range(1, nx):
        src = at_x(nx - d)
        remote(gains.at[src], gains.at[src], xg_s.at[d], xg_r.at[d], {"x": src}).wait_recv()
    for k in range(nx):
        block = sres[:, k * kw : (k + 1) * kw].astype(F32)
        nrm[:, k * kw : (k + 1) * kw] = (block * inverse * gains[k]).astype(BF16)

    local[2].wait()
    for d in range(1, nx):
        src = at_x(nx - d)
        remote(wq_part(src), wq.at[src], xw_s.at[d], xw_r.at[d], {"x": src}).wait_recv()

    @pl.when(x != 0)
    def _():
        remote(kvs.at[0], kvw.at[0], kv_s.at[0], kv_r.at[0], {"x": x // 2}).wait_recv()

    @pl.when(x != nx - 1)
    def _():
        remote(kvs.at[0], kvw.at[1], kv_s.at[0], kv_r.at[1], {"x": x // 2}).wait_recv()

    total = dot(nrm[:, :kw], wq[0])
    for k in range(1, nx):
        total = total + dot(nrm[:, k * kw : (k + 1) * kw], wq[k])
    part[:, :, :qcols] = total.reshape(nz, per_z, qcols)
    half = nrm[:, pl.ds(pl.multiple_of(lax.rem(x, 2) * 2 * kw, 2 * kw), 2 * kw)]
    kv_part = dot(half[:, :kw], kvw[0]) + dot(half[:, kw:], kvw[1])
    part[:, :, qcols:] = kv_part.reshape(nz, per_z, HD)

    right, left = {"z": at_z(1)}, {"z": at_z(nz - 1)}
    r_steps, l_steps = nz // 2, nz - 1 - nz // 2
    cols = part.shape[2]
    cuts = [(0, 384), (384, cols)]

    def r_copy(s, c):
        lo, hi = cuts[c]
        owner = at_z(r_steps - s)
        src = part.at[owner, :, lo:hi] if s == 0 else rbuf.at[s - 1, :, lo:hi]
        return remote(src, rbuf.at[s, :, lo:hi], rr_s.at[s, c], rr_r.at[s, c], right)

    def l_copy(s, c):
        lo, hi = cuts[c]
        owner = at_z(nz - l_steps + s)
        src = part.at[owner, :, lo:hi] if s == 0 else lbuf.at[s - 1, :, lo:hi]
        return remote(src, lbuf.at[s, :, lo:hi], lr_s.at[s, c], lr_r.at[s, c], left)

    for c in range(len(cuts)):
        send(r_copy(0, c))
        if l_steps > 0:
            send(l_copy(0, c))
    for s in range(r_steps):
        for c, (lo, hi) in enumerate(cuts):
            r_copy(s, c).wait_recv()
            if s + 1 < r_steps:
                owner = at_z(r_steps - s - 1)
                rbuf[s, :, lo:hi] = rbuf[s, :, lo:hi] + part[owner, :, lo:hi]
                send(r_copy(s + 1, c))
            if s < l_steps:
                l_copy(s, c).wait_recv()
                if s + 1 < l_steps:
                    owner = at_z(nz - l_steps + s + 1)
                    lbuf[s, :, lo:hi] = lbuf[s, :, lo:hi] + part[owner, :, lo:hi]
                    send(l_copy(s + 1, c))
    own = part[z] + rbuf[r_steps - 1]
    if l_steps > 0:
        own = own + lbuf[l_steps - 1]
    for k in range(nx):
        xs[k] = own[k * slots : (k + 1) * slots]
    for d in range(1, nx):
        send(remote(xs.at[at_x(d)], xin.at[x], xe_s.at[d], xe_r.at[d], {"x": at_x(d)}))
    xin[x] = xs[x]

    local[5].wait()
    lengths = [lens[asg[w_own * slots + j]] for j in range(slots)]
    angles = jnp.concatenate([tab[pl.ds(lengths[j], 1), :] for j in range(slots)], axis=0)
    turned = pltpu.roll(angles, HD // 2, 1)
    lane = lax.broadcasted_iota(jnp.int32, (slots, HD), 1)
    cosine = jnp.where(lane < HD // 2, angles, turned)
    sine = jnp.where(lane < HD // 2, -turned, angles)

    def rotate(v):
        return (v * cosine + pltpu.roll(v, HD // 2, 1) * sine).astype(BF16).astype(F32)

    for d in range(1, nx):
        src = at_x(nx - d)
        remote(xs.at[0], xin.at[src], xe_s.at[d], xe_r.at[d], {"x": src}).wait_recv()
    for k in range(nx):
        for i in range(heads_x):
            turned_query = rotate(xin[k, :, i * HD : (i + 1) * HD])
            for j in range(slots):
                q_ref[j, k * heads_x + i : k * heads_x + i + 1, :] = turned_query[j : j + 1]
    keys_new = rotate(xin[0, :, qcols:] + xin[1, :, qcols:])
    values_new = (xin[2, :, qcols:] + xin[3, :, qcols:]).astype(BF16).astype(F32)

    scale = 1.0 / math.sqrt(HD)
    position = lax.broadcasted_iota(jnp.int32, (heads, most), 1)
    for j in range(slots):
        query = q_ref[j]
        own_score = jnp.sum(query * keys_new[j : j + 1], axis=1, keepdims=True) * scale
        scores = dot_t(query.astype(BF16), kc[j]) * scale
        scores = jnp.where(position < lengths[j], scores, -jnp.inf)
        top = jnp.maximum(jnp.max(scores, axis=1, keepdims=True), own_score)
        weights = jnp.exp(scores - top)
        own_weight = jnp.exp(own_score - top)
        totals = jnp.sum(weights, axis=1, keepdims=True) + own_weight
        probs = (weights / totals).astype(BF16)
        own_prob = (own_weight / totals).astype(BF16).astype(F32)
        attended = dot(probs, vc[j]) + own_prob * values_new[j : j + 1]
        for h in range(heads):
            ab[j : j + 1, h * HD : (h + 1) * HD] = attended[h : h + 1]
    ag[w_own] = ab[...].astype(BF16)

    for d in reversed(by_distance(nz)):
        send(remote(ag.at[w_own], ag.at[w_own], az_s.at[d], az_r.at[d], {"z": at_z(d)}))
    for d in [0] + by_distance(nz):
        src_z = at_z(nz - d)
        block = x * nz + src_z
        if d > 0:
            remote(ag.at[block], ag.at[block], az_s.at[d], az_r.at[d], {"z": src_z}).wait_recv()
        for e in range(1, nx):
            send(remote(ag.at[block], ag.at[block], ax_s.at[d, e], ax_r.at[d, e], {"x": at_x(e)}))
    local[4].wait()
    for d in [0] + by_distance(nz):
        for e in range(1, nx):
            src_x = at_x(nx - e)
            block = src_x * nz + at_z(nz - d)
            remote(ag.at[block], ag.at[block], ax_s.at[d, e], ax_r.at[d, e], {"x": src_x}).wait_recv()

    group = 16 // slots
    for g in range(rows // 16):
        pieces = [ag[g * group + i].astype(F32) for i in range(group)]
        att[g * 16 : (g + 1) * 16, :] = jnp.concatenate(pieces, axis=0).astype(BF16)
    tile = 512
    update = jnp.zeros((rows, wo.shape[1]), F32)
    for k in range(att.shape[1] // tile):
        picked = dot(pr[...], att[:, k * tile : (k + 1) * tile]).astype(BF16)
        update = update + dot(picked, wo[k * tile : (k + 1) * tile, :])
    nst[...] = update.reshape(nn, rows_n, wo.shape[1])
    for d in range(1, nn):
        send(remote(nst.at[at_n(d)], nin.at[n], no_s.at[d], no_r.at[d], {"narrow": at_n(d)}))
    nin[n] = nst[n]
    for d in range(1, nn):
        src = at_n(nn - d)
        remote(nst.at[0], nin.at[src], no_s.at[d], no_r.at[d], {"narrow": src}).wait_recv()
    result = nin[0]
    for k in range(1, nn):
        result = result + nin[k]
    out_ref[...] = (nres[n, x].astype(F32) + result).astype(BF16)

    for copy in sends:
        copy.wait_send()

    @pl.when(x != 0)
    def _():
        k_copy.wait_send()

    @pl.when(x != nx - 1)
    def _():
        v_copy.wait_send()


def per_device(nx, nz, nn, table, residual, norm_gain, w_query, w_keyval, w_out, cache_rows, lengths, assignment):
    slots, most, _, channels = cache_rows.shape
    kw, query_cols = w_query.shape
    rows_n = residual.shape[0]
    rows = rows_n * nn
    qcols = query_cols // nx
    cols = qcols + HD
    heads = query_cols // HD
    r_steps, l_steps = nz // 2, max(nz - 1 - nz // 2, 1)
    width = kw * nx * nz
    anywhere = pl.BlockSpec(memory_space=pl.ANY)
    vmem = pl.BlockSpec(memory_space=pltpu.VMEM)
    smem = pl.BlockSpec(memory_space=pltpu.SMEM)
    dma = pltpu.SemaphoreType.DMA
    scratch = [
        pltpu.VMEM((nn, nx, rows_n, kw), BF16),
        pltpu.VMEM((nx, 1, kw), F32),
        pltpu.VMEM((nx, kw, qcols), BF16),
        pltpu.VMEM((2 * kw, HD), BF16),
        pltpu.VMEM((2, kw, HD), BF16),
        pltpu.VMEM((2, kw, HD), BF16),
        pltpu.VMEM(w_out.shape, BF16),
        pltpu.VMEM((slots * most * 2, HD), BF16),
        pltpu.VMEM((slots, most, HD), BF16),
        pltpu.VMEM((slots, most, HD), BF16),
        pltpu.VMEM(table.shape, F32),
        pltpu.VMEM((nz, 1, rows), F32),
        pltpu.VMEM((nn, 1, rows), F32),
        pltpu.VMEM((rows, rows), BF16),
        pltpu.VMEM((rows, rows), BF16),
        pltpu.VMEM((rows, nx * kw), BF16),
        pltpu.VMEM((rows, nx * kw), BF16),
        pltpu.VMEM((nz, nx * slots, cols), F32),
        pltpu.VMEM((r_steps, nx * slots, cols), F32),
        pltpu.VMEM((l_steps, nx * slots, cols), F32),
        pltpu.VMEM((nx, slots, cols), F32),
        pltpu.VMEM((nx, slots, cols), F32),
        pltpu.VMEM((slots, heads, HD), F32),
        pltpu.VMEM((slots, query_cols), F32),
        pltpu.VMEM((nx * nz, slots, query_cols), BF16),
        pltpu.VMEM((rows, query_cols), BF16),
        pltpu.VMEM((nn, rows_n, w_out.shape[1]), F32),
        pltpu.VMEM((nn, rows_n, w_out.shape[1]), F32),
        dma((6,)),
        dma((nx,)), dma((nx,)), dma((nx,)), dma((nx,)), dma((nx,)), dma((nx,)),
        dma((2,)), dma((2,)),
        dma((nn,)), dma((nn,)),
        dma((nz,)), dma((nz,)),
        dma((nn,)), dma((nn,)),
        dma((r_steps, 2)), dma((r_steps, 2)), dma((l_steps, 2)), dma((l_steps, 2)),
        dma((nx,)), dma((nx,)),
        dma((nz,)), dma((nz,)), dma((nz, nx)), dma((nz, nx)),
        dma((nn,)), dma((nn,)),
    ]
    return pl.pallas_call(
        functools.partial(kernel, nx, nz, nn, width),
        out_shape=jax.ShapeDtypeStruct(residual.shape, BF16),
        in_specs=[smem, smem, anywhere, vmem, vmem] + [anywhere] * 5,
        out_specs=vmem,
        scratch_shapes=scratch,
        compiler_params=pltpu.CompilerParams(
            collective_id=0, has_side_effects=True, vmem_limit_bytes=60 * 1024 * 1024
        ),
        name="decode_block",
    )(
        lengths,
        assignment,
        residual,
        norm_gain.reshape(1, -1),
        assignment.reshape(1, -1),
        w_query,
        w_keyval.reshape(2 * kw, channels),
        w_out,
        cache_rows.reshape(slots * most * 2, channels),
        table,
    )


def solution(mesh):
    nx, nn = 4, mesh.shape["narrow"]
    nz = mesh.shape["wide"] // nx
    torus = Mesh(mesh.devices.reshape(nx, nz, nn), ("x", "z", "narrow"))
    wide = ("x", "z")

    def run(residual, norm_gain, w_query, w_keyval, w_out, cache_rows, lengths, assignment):
        table = jnp.asarray(rotation_table(cache_rows.shape[1]))
        body = jax.shard_map(
            lambda table, *args: per_device(nx, nz, nn, table, *args),
            mesh=torus,
            in_specs=(
                P(),
                P("narrow", wide),
                P(wide),
                P(wide, "narrow"),
                P(wide, None, "narrow"),
                P("narrow", wide),
                P(wide, None, None, "narrow"),
                P(),
                P(),
            ),
            out_specs=P("narrow", wide),
            check_vma=False,
        )
        return body(table, residual, norm_gain, w_query, w_keyval, w_out, cache_rows, lengths, assignment)

    return run
```

```python
import functools
import math

import jax
import jax.numpy as jnp
import numpy as np
from jax import lax
from jax.experimental import pallas as pl
from jax.experimental.pallas import tpu as pltpu
from jax.sharding import Mesh
from jax.sharding import PartitionSpec as P

HD = 128
MESH = pl.DeviceIdType.MESH
F32 = jnp.float32
BF16 = jnp.bfloat16


def rotation_table(most):
    half = HD // 2
    exponents = -(np.arange(half, dtype=np.float32) * np.float32(2.0) / np.float32(HD))
    freqs = np.power(np.float32(500000.0), exponents).astype(np.float32)
    rows = (most + 8) // 8 * 8
    angles = (np.arange(rows, dtype=np.float32)[:, None] * freqs[None, :]).astype(np.float32)
    angles = angles.astype(np.float64)
    return np.concatenate([np.cos(angles), np.sin(angles)], axis=1).astype(np.float32)


def dot(a, b):
    return lax.dot_general(a, b, (((1,), (0,)), ((), ())), preferred_element_type=F32)


def dot_t(a, b):
    return lax.dot_general(a, b, (((1,), (1,)), ((), ())), preferred_element_type=F32)


def by_distance(count):
    return sorted(range(1, count), key=lambda d: min(d, count - d))


def kernel(
    nx, nz, nn, width,
    lens, asg, res_h, gain_h, asg_ref, wq_h, wkv_h, wo_h, cache_h, tab_h,
    out_ref,
    nres, gains, wq, wkv, kvs, kvw, wo, cache, kc, vc, tab,
    gain_v, zin, nsq, pz, pr, sres, nrm, part, rbuf, lbuf, xs, xin, q_ref, ab, ag, att, nst, nin,
    loc, xr_s, xr_r, xg_s, xg_r, xw_s, xw_r, kv_s, kv_r, ng_s, ng_r,
    zs_s, zs_r, ns_s, ns_r, rr_s, rr_r, lr_s, lr_r, xe_s, xe_r,
    az_s, az_r, ax_s, ax_r, no_s, no_r,
):
    x, z, n = lax.axis_index("x"), lax.axis_index("z"), lax.axis_index("narrow")
    y, c = n // 2, n % 2
    ny = nn // 2
    turn = 1 - 2 * c
    rows = pz.shape[0]
    rows_n = rows // nn
    slots = xs.shape[2]
    per_z = nx * slots
    pieces = part.shape[1]
    qcols = wq.shape[2]
    kw = wq.shape[1]
    most = kc.shape[1]
    heads = q_ref.shape[1]
    heads_x = heads // nx
    w_own = x * nz + z

    def remote(src, dst, ss, rs, dev):
        return pltpu.make_async_remote_copy(
            src_ref=src, dst_ref=dst, send_sem=ss, recv_sem=rs, device_id=dev, device_id_type=MESH
        )

    def at_x(d):
        return lax.rem(x + d, nx)

    def at_z(d):
        return lax.rem(z + d, nz)

    def at_n(d):
        return lax.rem(n + d, nn)

    def wq_part(t):
        return wq_h.at[:, pl.ds(pl.multiple_of(t * qcols, qcols), qcols)]

    plane = [(dx, dn) for dx in range(nx) for dn in range(nn) if dx + dn > 0]
    local = [
        pltpu.make_async_copy(wkv_h, wkv, loc.at[0]),
        pltpu.make_async_copy(res_h, nres.at[n, x], loc.at[1]),
        pltpu.make_async_copy(wq_part(x), wq.at[x], loc.at[2]),
        pltpu.make_async_copy(cache_h, cache, loc.at[3]),
        pltpu.make_async_copy(wo_h, wo, loc.at[4]),
        pltpu.make_async_copy(tab_h, tab, loc.at[5]),
        pltpu.make_async_copy(gain_h, gain_v, loc.at[6]),
    ]
    barrier = pltpu.get_barrier_semaphore()
    for d in reversed(by_distance(nz)):
        pl.semaphore_signal(barrier, inc=1, device_id={"z": at_z(d)}, device_id_type=MESH)
    for dx, dn in plane:
        dev = {"x": at_x(dx), "narrow": at_n(dn)}
        pl.semaphore_signal(barrier, inc=1, device_id=dev, device_id_type=MESH)
    for copy in local:
        copy.start()

    a_row = asg_ref[...]
    i_sub = lax.broadcasted_iota(jnp.int32, (rows, rows), 0)
    i_lane = lax.broadcasted_iota(jnp.int32, (rows, rows), 1)
    zz, rest = i_sub // per_z, i_sub % per_z
    slot_of = ((rest // slots) * nz + zz) * slots + rest % slots
    a_col = jnp.sum(
        jnp.where(i_lane == slot_of, a_row.astype(F32), 0.0), axis=1, keepdims=True
    ).astype(jnp.int32)
    pick = i_lane == a_col
    pz[...] = jnp.where(pick, 1.0, 0.0).astype(BF16)
    pr[...] = jnp.where(i_sub == a_row, 1.0, 0.0).astype(BF16)
    local[6].wait()
    gains[x] = gain_v[...].astype(F32).reshape(1, kw)

    local[1].wait()
    block = nres[n, x].astype(F32)
    squares = jnp.sum(block * block, axis=1, keepdims=True)
    r_sub = lax.broadcasted_iota(jnp.int32, (rows_n, rows), 0)
    r_lane = lax.broadcasted_iota(jnp.int32, (rows_n, rows), 1)
    zin[z] = jnp.sum(jnp.where(r_lane == r_sub + n * rows_n, squares, 0.0), axis=0, keepdims=True)

    e_row = lax.broadcasted_iota(jnp.int32, (kw, 2 * kw), 0)
    e_col = lax.broadcasted_iota(jnp.int32, (kw, 2 * kw), 1)
    e0 = jnp.where(e_col == 2 * e_row, 1.0, 0.0).astype(BF16)
    e1 = jnp.where(e_col == 2 * e_row + 1, 1.0, 0.0).astype(BF16)
    local[0].wait()
    kvs[0] = dot(e0, wkv[...]).astype(BF16)
    kvs[1] = dot(e1, wkv[...]).astype(BF16)

    pl.semaphore_wait(barrier, len(plane) + nz - 1)

    sends = []

    def send(copy):
        copy.start()
        sends.append(copy)

    for d in reversed(by_distance(nz)):
        send(remote(zin.at[z], zin.at[z], zs_s.at[d], zs_r.at[d], {"z": at_z(d)}))
    for d in range(1, nx):
        dev = {"x": at_x(d)}
        send(remote(res_h, nres.at[n, x], xr_s.at[d], xr_r.at[d], dev))
        send(remote(gains.at[x], gains.at[x], xg_s.at[d], xg_r.at[d], dev))
    for d in range(1, nx):
        send(remote(wq_part(at_x(d)), wq.at[x], xw_s.at[d], xw_r.at[d], {"x": at_x(d)}))
    kv_slot = lax.rem(x, 2)
    k_copy = remote(kvs.at[0], kvw.at[kv_slot], kv_s.at[0], kv_r.at[kv_slot], {"x": x // 2})
    v_copy = remote(kvs.at[1], kvw.at[kv_slot], kv_s.at[1], kv_r.at[kv_slot], {"x": 2 + x // 2})

    @pl.when(x != 0)
    def _():
        k_copy.start()

    @pl.when(x == 0)
    def _():
        kvw[0] = kvs[0]

    @pl.when(x != nx - 1)
    def _():
        v_copy.start()

    @pl.when(x == nx - 1)
    def _():
        kvw[1] = kvs[1]

    def narrow(dy, core):
        return lax.rem(y + dy + ny, ny) * 2 + core

    def row_copy(k, src, to):
        return remote(nres.at[src], nres.at[src], ng_s.at[k], ng_r.at[k], {"narrow": to})

    for d in range(1, nx):
        src = at_x(nx - d)
        remote(res_h, nres.at[n, src], xr_s.at[d], xr_r.at[d], {"x": src}).wait_recv()
    ahead, behind, across = narrow(turn, c), narrow(-turn, c), narrow(2, c)
    other = narrow(0, 1 - c)
    send(row_copy(0, n, ahead))
    send(row_copy(1, n, behind))
    send(row_copy(3, n, other))

    local[3].wait()
    step = kw
    for j in range(slots):
        for b in range(most // step):
            block = cache[pl.ds((j * most + b * step) * 2, 2 * step), :]
            kc[j, b * step : (b + 1) * step, :] = dot(e0, block).astype(BF16)
            vc[j, b * step : (b + 1) * step, :] = dot(e1, block).astype(BF16)

    row_copy(0, behind, behind).wait_recv()
    send(row_copy(2, behind, ahead))
    send(row_copy(4, behind, other))
    row_copy(1, ahead, ahead).wait_recv()
    send(row_copy(5, ahead, other))

    for d in range(1, nz):
        src = at_z(nz - d)
        remote(zin.at[src], zin.at[src], zs_s.at[d], zs_r.at[d], {"z": src}).wait_recv()
    nsq[x, n] = jnp.sum(zin[...], axis=0)
    for dx, dn in plane:
        dev = {"x": at_x(dx), "narrow": at_n(dn)}
        send(remote(nsq.at[x, n], nsq.at[x, n], ns_s.at[dx, dn], ns_r.at[dx, dn], dev))

    row_copy(2, across, behind).wait_recv()
    send(row_copy(6, across, other))
    far = narrow(-2 * turn, 1 - c)
    for k, src in ((3, other), (4, narrow(turn, 1 - c)), (5, narrow(-turn, 1 - c)), (6, far)):
        row_copy(k, src, other).wait_recv()
    for k in range(nx):
        block = nres[:, k].reshape(rows, kw)
        sres[:, k * kw : (k + 1) * kw] = dot(pz[...], block).astype(BF16)

    for dx, dn in plane:
        src = (at_x(nx - dx), at_n(nn - dn))
        dev = {"x": src[0], "narrow": src[1]}
        remote(nsq.at[src], nsq.at[src], ns_s.at[dx, dn], ns_r.at[dx, dn], dev).wait_recv()
    sums = jnp.sum(nsq[...].reshape(nx * nn, 1, rows), axis=0)
    sum_col = jnp.sum(jnp.where(pz[...].astype(F32) > 0.5, sums, 0.0), axis=1, keepdims=True)
    inverse = lax.rsqrt(sum_col / width + 1e-05)

    for d in range(1, nx):
        src = at_x(nx - d)
        remote(gains.at[src], gains.at[src], xg_s.at[d], xg_r.at[d], {"x": src}).wait_recv()
    for k in range(nx):
        block = sres[:, k * kw : (k + 1) * kw].astype(F32)
        nrm[:, k * kw : (k + 1) * kw] = (block * inverse * gains[k]).astype(BF16)

    local[2].wait()
    for d in range(1, nx):
        src = at_x(nx - d)
        remote(wq_part(src), wq.at[src], xw_s.at[d], xw_r.at[d], {"x": src}).wait_recv()

    @pl.when(x != 0)
    def _():
        remote(kvs.at[0], kvw.at[0], kv_s.at[0], kv_r.at[0], {"x": x // 2}).wait_recv()

    @pl.when(x != nx - 1)
    def _():
        remote(kvs.at[0], kvw.at[1], kv_s.at[0], kv_r.at[1], {"x": x // 2}).wait_recv()

    total = dot(nrm[:, :kw], wq[0])
    for k in range(1, nx):
        total = total + dot(nrm[:, k * kw : (k + 1) * kw], wq[k])
    for k in range(pieces - 1):
        part[:, k] = total[:, k * HD : (k + 1) * HD].reshape(nz, per_z, HD)
    half = nrm[:, pl.ds(pl.multiple_of(lax.rem(x, 2) * 2 * kw, 2 * kw), 2 * kw)]
    kv_part = dot(half[:, :kw], kvw[0]) + dot(half[:, kw:], kvw[1])
    part[:, pieces - 1] = kv_part.reshape(nz, per_z, HD)

    right, left = {"z": at_z(1)}, {"z": at_z(nz - 1)}
    r_steps, l_steps = nz // 2, nz - 1 - nz // 2

    def r_copy(s, k):
        src = part.at[at_z(r_steps), k] if s == 0 else rbuf.at[s - 1, k]
        return remote(src, rbuf.at[s, k], rr_s.at[s, k], rr_r.at[s, k], right)

    def l_copy(s, k):
        src = part.at[at_z(nz - l_steps), k] if s == 0 else lbuf.at[s - 1, k]
        return remote(src, lbuf.at[s, k], lr_s.at[s, k], lr_r.at[s, k], left)

    for k in range(pieces):
        send(r_copy(0, k))
        send(l_copy(0, k))
    for s in range(r_steps):
        for k in range(pieces):
            r_copy(s, k).wait_recv()
            if s + 1 < r_steps:
                rbuf[s, k] = rbuf[s, k] + part[at_z(r_steps - s - 1), k]
                send(r_copy(s + 1, k))
            else:
                own = part[z, k] + rbuf[s, k] + lbuf[l_steps - 1, k]
                for t in range(nx):
                    xs[t, k] = own[t * slots : (t + 1) * slots]
                for d in range(1, nx):
                    to = at_x(d)
                    send(remote(xs.at[to, k], xin.at[x, k], xe_s.at[d, k], xe_r.at[d, k], {"x": to}))
            if s < l_steps:
                l_copy(s, k).wait_recv()
                if s + 1 < l_steps:
                    lbuf[s, k] = lbuf[s, k] + part[at_z(nz - l_steps + s + 1), k]
                    send(l_copy(s + 1, k))
    xin[x] = xs[x]

    local[5].wait()
    lengths = [lens[asg[w_own * slots + j]] for j in range(slots)]
    angles = jnp.concatenate([tab[pl.ds(lengths[j], 1), :] for j in range(slots)], axis=0)
    turned = pltpu.roll(angles, HD // 2, 1)
    lane = lax.broadcasted_iota(jnp.int32, (slots, HD), 1)
    cosine = jnp.where(lane < HD // 2, angles, turned)
    sine = jnp.where(lane < HD // 2, -turned, angles)

    def rotate(v):
        return (v * cosine + pltpu.roll(v, HD // 2, 1) * sine).astype(BF16).astype(F32)

    for k in range(pieces):
        for d in range(1, nx):
            src = at_x(nx - d)
            remote(xs.at[0, k], xin.at[src, k], xe_s.at[d, k], xe_r.at[d, k], {"x": src}).wait_recv()
    for k in range(nx):
        for i in range(heads_x):
            turned_query = rotate(xin[k, i])
            for j in range(slots):
                q_ref[j, k * heads_x + i : k * heads_x + i + 1, :] = turned_query[j : j + 1]
    keys_new = rotate(xin[0, pieces - 1] + xin[1, pieces - 1])
    values_new = (xin[2, pieces - 1] + xin[3, pieces - 1]).astype(BF16).astype(F32)

    scale = 1.0 / math.sqrt(HD)
    position = lax.broadcasted_iota(jnp.int32, (heads, most), 1)
    for j in range(slots):
        query = q_ref[j]
        own_score = jnp.sum(query * keys_new[j : j + 1], axis=1, keepdims=True) * scale
        scores = dot_t(query.astype(BF16), kc[j]) * scale
        scores = jnp.where(position < lengths[j], scores, -jnp.inf)
        top = jnp.maximum(jnp.max(scores, axis=1, keepdims=True), own_score)
        weights = jnp.exp(scores - top)
        own_weight = jnp.exp(own_score - top)
        totals = jnp.sum(weights, axis=1, keepdims=True) + own_weight
        probs = (weights / totals).astype(BF16)
        own_prob = (own_weight / totals).astype(BF16).astype(F32)
        attended = dot(probs, vc[j]) + own_prob * values_new[j : j + 1]
        for h in range(heads):
            ab[j : j + 1, h * HD : (h + 1) * HD] = attended[h : h + 1]
    ag[w_own] = ab[...].astype(BF16)

    reach = nz // 4

    def z_copy(d, block, to):
        return remote(ag.at[block], ag.at[block], az_s.at[d], az_r.at[d], {"z": to})

    def x_copy(d, e, block, to):
        return remote(ag.at[block], ag.at[block], ax_s.at[d, e], ax_r.at[d, e], {"x": to})

    def block_of(e, d):
        return at_x(nx - e) * nz + at_z(nz - d)

    for k in range(reach, 0, -1):
        send(z_copy(k, w_own, at_z(k)))
        send(z_copy(nz - k, w_own, at_z(nz - k)))
    order = [0] + by_distance(nz)
    lag = 4
    for step in range(len(order) + lag):
        if step < len(order):
            d = order[step]
            block = block_of(0, d)
            if d > 0:
                z_copy(d, block, z).wait_recv()
            if d == reach:
                for k in range(1, reach + 1):
                    send(z_copy(reach + k, block, at_z(k)))
            if d == nz - reach:
                for k in range(1, reach):
                    send(z_copy(nz - reach - k, block, at_z(nz - k)))
            send(x_copy(d, 1, block, at_x(1)))
            send(x_copy(d, nx - 1, block, at_x(nx - 1)))
        if step >= lag:
            d = order[step - lag]
            e = 1 if d % 2 == 0 else nx - 1
            block = block_of(e, d)
            x_copy(d, e, block, x).wait_recv()
            send(x_copy(d, 2, block, at_x(e)))
    local[4].wait()
    for d in order:
        for e in (nx - 1 if d % 2 == 0 else 1, 2):
            x_copy(d, e, block_of(e, d), x).wait_recv()

    group = 16 // slots
    for g in range(rows // 16):
        blocks = [ag[g * group + i].astype(F32) for i in range(group)]
        att[g * 16 : (g + 1) * 16, :] = jnp.concatenate(blocks, axis=0).astype(BF16)
    tile = 512
    update = jnp.zeros((rows, wo.shape[1]), F32)
    for k in range(att.shape[1] // tile):
        picked = dot(pr[...], att[:, k * tile : (k + 1) * tile]).astype(BF16)
        update = update + dot(picked, wo[k * tile : (k + 1) * tile, :])
    nst[...] = update.reshape(nn, rows_n, wo.shape[1])
    for d in range(1, nn):
        send(remote(nst.at[at_n(d)], nin.at[n], no_s.at[d], no_r.at[d], {"narrow": at_n(d)}))
    nin[n] = nst[n]
    for d in range(1, nn):
        src = at_n(nn - d)
        remote(nst.at[0], nin.at[src], no_s.at[d], no_r.at[d], {"narrow": src}).wait_recv()
    result = nin[0]
    for k in range(1, nn):
        result = result + nin[k]
    out_ref[...] = (nres[n, x].astype(F32) + result).astype(BF16)

    for copy in sends:
        copy.wait_send()

    @pl.when(x != 0)
    def _():
        k_copy.wait_send()

    @pl.when(x != nx - 1)
    def _():
        v_copy.wait_send()


def per_device(nx, nz, nn, table, residual, norm_gain, w_query, w_keyval, w_out, cache_rows, lengths, assignment):
    slots, most, _, channels = cache_rows.shape
    kw, query_cols = w_query.shape
    rows_n = residual.shape[0]
    rows = rows_n * nn
    qcols = query_cols // nx
    pieces = qcols // HD + 1
    heads = query_cols // HD
    r_steps, l_steps = nz // 2, max(nz - 1 - nz // 2, 1)
    width = kw * nx * nz
    anywhere = pl.BlockSpec(memory_space=pl.ANY)
    vmem = pl.BlockSpec(memory_space=pltpu.VMEM)
    smem = pl.BlockSpec(memory_space=pltpu.SMEM)
    dma = pltpu.SemaphoreType.DMA
    scratch = [
        pltpu.VMEM((nn, nx, rows_n, kw), BF16),
        pltpu.VMEM((nx, 1, kw), F32),
        pltpu.VMEM((nx, kw, qcols), BF16),
        pltpu.VMEM((2 * kw, HD), BF16),
        pltpu.VMEM((2, kw, HD), BF16),
        pltpu.VMEM((2, kw, HD), BF16),
        pltpu.VMEM(w_out.shape, BF16),
        pltpu.VMEM((slots * most * 2, HD), BF16),
        pltpu.VMEM((slots, most, HD), BF16),
        pltpu.VMEM((slots, most, HD), BF16),
        pltpu.VMEM(table.shape, F32),
        pltpu.VMEM((kw,), BF16),
        pltpu.VMEM((nz, 1, rows), F32),
        pltpu.VMEM((nx, nn, 1, rows), F32),
        pltpu.VMEM((rows, rows), BF16),
        pltpu.VMEM((rows, rows), BF16),
        pltpu.VMEM((rows, nx * kw), BF16),
        pltpu.VMEM((rows, nx * kw), BF16),
        pltpu.VMEM((nz, pieces, nx * slots, HD), F32),
        pltpu.VMEM((r_steps, pieces, nx * slots, HD), F32),
        pltpu.VMEM((l_steps, pieces, nx * slots, HD), F32),
        pltpu.VMEM((nx, pieces, slots, HD), F32),
        pltpu.VMEM((nx, pieces, slots, HD), F32),
        pltpu.VMEM((slots, heads, HD), F32),
        pltpu.VMEM((slots, query_cols), F32),
        pltpu.VMEM((nx * nz, slots, query_cols), BF16),
        pltpu.VMEM((rows, query_cols), BF16),
        pltpu.VMEM((nn, rows_n, w_out.shape[1]), F32),
        pltpu.VMEM((nn, rows_n, w_out.shape[1]), F32),
        dma((7,)),
        dma((nx,)), dma((nx,)), dma((nx,)), dma((nx,)), dma((nx,)), dma((nx,)),
        dma((2,)), dma((2,)),
        dma((7,)), dma((7,)),
        dma((nz,)), dma((nz,)),
        dma((nx, nn)), dma((nx, nn)),
        dma((r_steps, pieces)), dma((r_steps, pieces)), dma((l_steps, pieces)), dma((l_steps, pieces)),
        dma((nx, pieces)), dma((nx, pieces)),
        dma((nz,)), dma((nz,)), dma((nz, nx)), dma((nz, nx)),
        dma((nn,)), dma((nn,)),
    ]
    return pl.pallas_call(
        functools.partial(kernel, nx, nz, nn, width),
        out_shape=jax.ShapeDtypeStruct(residual.shape, BF16),
        in_specs=[smem, smem, anywhere, anywhere, vmem] + [anywhere] * 5,
        out_specs=vmem,
        scratch_shapes=scratch,
        compiler_params=pltpu.CompilerParams(
            collective_id=0, has_side_effects=True, vmem_limit_bytes=60 * 1024 * 1024
        ),
        name="decode_block",
    )(
        lengths,
        assignment,
        residual,
        norm_gain,
        assignment.reshape(1, -1),
        w_query,
        w_keyval.reshape(2 * kw, channels),
        w_out,
        cache_rows.reshape(slots * most * 2, channels),
        table,
    )


def solution(mesh):
    nx, nn = 4, mesh.shape["narrow"]
    nz = mesh.shape["wide"] // nx
    torus = Mesh(mesh.devices.reshape(nx, nz, nn), ("x", "z", "narrow"))
    wide = ("x", "z")

    def run(residual, norm_gain, w_query, w_keyval, w_out, cache_rows, lengths, assignment):
        table = jnp.asarray(rotation_table(cache_rows.shape[1]))
        body = jax.shard_map(
            lambda table, *args: per_device(nx, nz, nn, table, *args),
            mesh=torus,
            in_specs=(
                P(),
                P("narrow", wide),
                P(wide),
                P(wide, "narrow"),
                P(wide, None, "narrow"),
                P("narrow", wide),
                P(wide, None, None, "narrow"),
                P(),
                P(),
            ),
            out_specs=P("narrow", wide),
            check_vma=False,
        )
        return body(table, residual, norm_gain, w_query, w_keyval, w_out, cache_rows, lengths, assignment)

    return run
```

```python
import functools
import math

import jax
import jax.numpy as jnp
import numpy as np
from jax import lax
from jax.experimental import pallas as pl
from jax.experimental.pallas import tpu as pltpu
from jax.sharding import Mesh
from jax.sharding import PartitionSpec as P

HD = 128
MESH = pl.DeviceIdType.MESH
F32 = jnp.float32
BF16 = jnp.bfloat16


def rotation_table(most):
    half = HD // 2
    exponents = -(np.arange(half, dtype=np.float32) * np.float32(2.0) / np.float32(HD))
    freqs = np.power(np.float32(500000.0), exponents).astype(np.float32)
    rows = (most + 8) // 8 * 8
    angles = (np.arange(rows, dtype=np.float32)[:, None] * freqs[None, :]).astype(np.float32)
    angles = angles.astype(np.float64)
    return np.concatenate([np.cos(angles), np.sin(angles)], axis=1).astype(np.float32)


def dot(a, b):
    return lax.dot_general(a, b, (((1,), (0,)), ((), ())), preferred_element_type=F32)


def dot_t(a, b):
    return lax.dot_general(a, b, (((1,), (1,)), ((), ())), preferred_element_type=F32)


def by_distance(count):
    return sorted(range(1, count), key=lambda d: min(d, count - d))


def kernel(
    nx, nz, nn, width,
    lens, asg, res_h, gain_h, asg_ref, wq_h, wkv_h, wo_h, cache_h, tab_h,
    out_ref,
    nres, gains, wq, wkv, kvs, kvw, wo, cache, kc, vc, tab,
    gain_v, zin, nsq, pz, pr, sres, nrm, part, r_even, r_odd, l_even, l_odd, wrel, xs, xin, q_ref, ab, ag, att, nst, nin,
    loc, xr_s, xr_r, xg_s, xg_r, xw_s, xw_r, kv_s, kv_r, ng_s, ng_r,
    zs_s, zs_r, ns_s, ns_r, re_s, re_r, ro_s, ro_r, le_s, le_r, lo_s, lo_r, wr_s, wr_r, wf_s, wf_r, xe_s, xe_r,
    az_s, az_r, ax_s, ax_r, no_s, no_r,
):
    x, z, n = lax.axis_index("x"), lax.axis_index("z"), lax.axis_index("narrow")
    y, c = n // 2, n % 2
    ny = nn // 2
    turn = 1 - 2 * c
    rows = pz.shape[0]
    rows_n = rows // nn
    slots = xs.shape[2]
    per_z = nx * slots
    pieces = part.shape[1]
    qcols = wq.shape[2]
    kw = wq.shape[1]
    most = kc.shape[1]
    heads = q_ref.shape[1]
    heads_x = heads // nx
    w_own = x * nz + z

    def remote(src, dst, ss, rs, dev):
        return pltpu.make_async_remote_copy(
            src_ref=src, dst_ref=dst, send_sem=ss, recv_sem=rs, device_id=dev, device_id_type=MESH
        )

    def at_x(d):
        return lax.rem(x + d, nx)

    def at_z(d):
        return lax.rem(z + d, nz)

    def at_n(d):
        return lax.rem(n + d, nn)

    def wq_part(t):
        return wq_h.at[:, pl.ds(pl.multiple_of(t * qcols, qcols), qcols)]

    local = [
        pltpu.make_async_copy(gain_h, gain_v, loc.at[6]),
        pltpu.make_async_copy(wkv_h, wkv, loc.at[0]),
        pltpu.make_async_copy(res_h, nres.at[n, x], loc.at[1]),
        pltpu.make_async_copy(wq_part(x), wq.at[x], loc.at[2]),
        pltpu.make_async_copy(cache_h, cache, loc.at[3]),
        pltpu.make_async_copy(wo_h, wo, loc.at[4]),
        pltpu.make_async_copy(tab_h, tab, loc.at[5]),
    ]
    barrier = pltpu.get_barrier_semaphore()
    for d in reversed(by_distance(nz)):
        pl.semaphore_signal(barrier, inc=1, device_id={"z": at_z(d)}, device_id_type=MESH)
    for d in range(1, nx):
        pl.semaphore_signal(barrier, inc=1, device_id={"x": at_x(d)}, device_id_type=MESH)
    for d in range(1, nn):
        pl.semaphore_signal(barrier, inc=1, device_id={"narrow": at_n(d)}, device_id_type=MESH)
    for copy in local:
        copy.start()
    gain_in, wkv_in, res_in, wq_in, cache_in, wo_in, tab_in = local
    pl.semaphore_wait(barrier, (nx - 1) + (nz - 1) + (nn - 1))

    sends = []

    def send(copy):
        copy.start()
        sends.append(copy)

    def relay_half(i, src, to):
        return remote(src, wrel.at[i], wr_s.at[i], wr_r.at[i], {"x": to})

    def relayed(i, owner, to):
        half = wq.at[owner, i * (kw // 2) : (i + 1) * (kw // 2)]
        return remote(wrel.at[i], half, wf_s.at[i], wf_r.at[i], {"x": to})

    for d in range(1, nx):
        send(remote(res_h, nres.at[n, x], xr_s.at[d], xr_r.at[d], {"x": at_x(d)}))
    gain_in.wait()
    gains[x] = gain_v[...].astype(F32).reshape(1, kw)
    for d in range(1, nx):
        send(remote(gains.at[x], gains.at[x], xg_s.at[d], xg_r.at[d], {"x": at_x(d)}))
    far_cols = pl.ds(pl.multiple_of(at_x(2) * qcols, qcols), qcols)
    send(relay_half(0, wq_h.at[0 : kw // 2, far_cols], at_x(1)))
    send(relay_half(1, wq_h.at[kw // 2 : kw, far_cols], at_x(nx - 1)))
    for d in (1, nx - 1):
        send(remote(wq_part(at_x(d)), wq.at[x], xw_s.at[d], xw_r.at[d], {"x": at_x(d)}))

    a_row = asg_ref[...]
    i_sub = lax.broadcasted_iota(jnp.int32, (rows, rows), 0)
    i_lane = lax.broadcasted_iota(jnp.int32, (rows, rows), 1)
    zz, rest = i_sub // per_z, i_sub % per_z
    slot_of = ((rest // slots) * nz + zz) * slots + rest % slots
    a_col = jnp.sum(
        jnp.where(i_lane == slot_of, a_row.astype(F32), 0.0), axis=1, keepdims=True
    ).astype(jnp.int32)
    pick = i_lane == a_col
    pz[...] = jnp.where(pick, 1.0, 0.0).astype(BF16)
    pr[...] = jnp.where(i_sub == a_row, 1.0, 0.0).astype(BF16)

    e_row = lax.broadcasted_iota(jnp.int32, (kw, 2 * kw), 0)
    e_col = lax.broadcasted_iota(jnp.int32, (kw, 2 * kw), 1)
    e0 = jnp.where(e_col == 2 * e_row, 1.0, 0.0).astype(BF16)
    e1 = jnp.where(e_col == 2 * e_row + 1, 1.0, 0.0).astype(BF16)
    wkv_in.wait()
    kvs[0] = dot(e0, wkv[...]).astype(BF16)
    kvs[1] = dot(e1, wkv[...]).astype(BF16)

    kv_slot = lax.rem(x, 2)
    k_copy = remote(kvs.at[0], kvw.at[kv_slot], kv_s.at[0], kv_r.at[kv_slot], {"x": x // 2})
    v_copy = remote(kvs.at[1], kvw.at[kv_slot], kv_s.at[1], kv_r.at[kv_slot], {"x": 2 + x // 2})

    @pl.when(x != 0)
    def _():
        k_copy.start()

    @pl.when(x == 0)
    def _():
        kvw[0] = kvs[0]

    @pl.when(x != nx - 1)
    def _():
        v_copy.start()

    @pl.when(x == nx - 1)
    def _():
        kvw[1] = kvs[1]

    def narrow(dy, core):
        return lax.rem(y + dy + ny, ny) * 2 + core

    def row_copy(k, src, to):
        return remote(nres.at[src], nres.at[src], ng_s.at[k], ng_r.at[k], {"narrow": to})

    res_in.wait()
    for d in range(1, nx):
        src = at_x(nx - d)
        remote(res_h, nres.at[n, src], xr_s.at[d], xr_r.at[d], {"x": src}).wait_recv()
    ahead, behind, across = narrow(turn, c), narrow(-turn, c), narrow(2, c)
    other = narrow(0, 1 - c)
    send(row_copy(0, n, ahead))
    send(row_copy(1, n, behind))
    send(row_copy(3, n, other))

    squares = jnp.zeros((rows_n, 1), F32)
    for k in range(nx):
        block = nres[n, k].astype(F32)
        squares = squares + jnp.sum(block * block, axis=1, keepdims=True)
    r_sub = lax.broadcasted_iota(jnp.int32, (rows_n, rows), 0)
    r_lane = lax.broadcasted_iota(jnp.int32, (rows_n, rows), 1)
    zin[z] = jnp.sum(jnp.where(r_lane == r_sub + n * rows_n, squares, 0.0), axis=0, keepdims=True)
    for d in reversed(by_distance(nz)):
        send(remote(zin.at[z], zin.at[z], zs_s.at[d], zs_r.at[d], {"z": at_z(d)}))

    cache_in.wait()
    step = kw
    for j in range(slots):
        for b in range(most // step):
            block = cache[pl.ds((j * most + b * step) * 2, 2 * step), :]
            kc[j, b * step : (b + 1) * step, :] = dot(e0, block).astype(BF16)
            vc[j, b * step : (b + 1) * step, :] = dot(e1, block).astype(BF16)

    left_x, right_x, opposite = at_x(nx - 1), at_x(1), at_x(2)
    relay_half(0, wrel.at[0], left_x).wait_recv()
    send(relayed(0, left_x, right_x))
    relay_half(1, wrel.at[1], right_x).wait_recv()
    send(relayed(1, right_x, left_x))

    row_copy(0, behind, behind).wait_recv()
    send(row_copy(2, behind, ahead))
    send(row_copy(4, behind, other))
    row_copy(1, ahead, ahead).wait_recv()
    send(row_copy(5, ahead, other))
    row_copy(2, across, behind).wait_recv()
    send(row_copy(6, across, other))

    for d in range(1, nz):
        src = at_z(nz - d)
        remote(zin.at[src], zin.at[src], zs_s.at[d], zs_r.at[d], {"z": src}).wait_recv()
    nsq[n] = jnp.sum(zin[...], axis=0)
    for d in range(1, nn):
        send(remote(nsq.at[n], nsq.at[n], ns_s.at[d], ns_r.at[d], {"narrow": at_n(d)}))

    far = narrow(-2 * turn, 1 - c)
    for k, src in ((3, other), (4, narrow(turn, 1 - c)), (5, narrow(-turn, 1 - c)), (6, far)):
        row_copy(k, src, other).wait_recv()
    for k in range(nx):
        block = nres[:, k].reshape(rows, kw)
        sres[:, k * kw : (k + 1) * kw] = dot(pz[...], block).astype(BF16)

    for d in range(1, nn):
        src = at_n(nn - d)
        remote(nsq.at[src], nsq.at[src], ns_s.at[d], ns_r.at[d], {"narrow": src}).wait_recv()
    sums = jnp.sum(nsq[...], axis=0)
    sum_col = jnp.sum(jnp.where(pz[...].astype(F32) > 0.5, sums, 0.0), axis=1, keepdims=True)
    inverse = lax.rsqrt(sum_col / width + 1e-05)

    for d in range(1, nx):
        src = at_x(nx - d)
        remote(gains.at[src], gains.at[src], xg_s.at[d], xg_r.at[d], {"x": src}).wait_recv()
    for k in range(nx):
        block = sres[:, k * kw : (k + 1) * kw].astype(F32)
        nrm[:, k * kw : (k + 1) * kw] = (block * inverse * gains[k]).astype(BF16)

    wq_in.wait()
    for d in (1, nx - 1):
        src = at_x(nx - d)
        remote(wq_part(src), wq.at[src], xw_s.at[d], xw_r.at[d], {"x": src}).wait_recv()
    relayed(0, opposite, left_x).wait_recv()
    relayed(1, opposite, right_x).wait_recv()

    @pl.when(x != 0)
    def _():
        remote(kvs.at[0], kvw.at[0], kv_s.at[0], kv_r.at[0], {"x": x // 2}).wait_recv()

    @pl.when(x != nx - 1)
    def _():
        remote(kvs.at[0], kvw.at[1], kv_s.at[0], kv_r.at[1], {"x": x // 2}).wait_recv()

    total = dot(nrm[:, :kw], wq[0])
    for k in range(1, nx):
        total = total + dot(nrm[:, k * kw : (k + 1) * kw], wq[k])
    for k in range(pieces - 1):
        part[:, k] = total[:, k * HD : (k + 1) * HD].reshape(nz, per_z, HD)
    half = nrm[:, pl.ds(pl.multiple_of(lax.rem(x, 2) * 2 * kw, 2 * kw), 2 * kw)]
    kv_part = dot(half[:, :kw], kvw[0]) + dot(half[:, kw:], kvw[1])
    part[:, pieces - 1] = kv_part.reshape(nz, per_z, HD)

    steps = nz // 4
    sides = ((1, r_even, r_odd, re_s, re_r, ro_s, ro_r), (-1, l_even, l_odd, le_s, le_r, lo_s, lo_r))

    def along(side, d):
        return at_z(d if side[0] > 0 else nz - d)

    def odd_copy(side, i, k):
        src = part.at[along(side, 2 * i + 1), k]
        to = {"z": along(side, 1)}
        return remote(src, side[2].at[i, k], side[5].at[i, k], side[6].at[i, k], to)

    def even_copy(side, s, k):
        if s == 0:
            src = part.at[along(side, 2 * steps), k]
        elif s == 1 and side[0] < 0:
            src = side[2].at[steps - 1, k]
        else:
            src = side[1].at[s - 1, k]
        to = {"z": along(side, 2)}
        return remote(src, side[1].at[s, k], side[3].at[s, k], side[4].at[s, k], to)

    for k in range(pieces):
        send(even_copy(sides[0], 0, k))
        for side in sides:
            send(odd_copy(side, steps - 1, k))
    for i in range(steps - 2, -1, -1):
        for k in range(pieces):
            for side in sides:
                send(odd_copy(side, i, k))
    for s in range(1, steps):
        for k in range(pieces):
            for side in sides:
                own_part = part[along(side, 2 * (steps - s)), k]
                odd_copy(side, steps - s, k).wait_recv()
                if s == 1 and side[0] < 0:
                    side[2][steps - 1, k] = side[2][steps - 1, k] + own_part
                else:
                    even_copy(side, s - 1, k).wait_recv()
                    side[1][s - 1, k] = side[1][s - 1, k] + side[2][steps - s, k] + own_part
                send(even_copy(side, s, k))
    for k in range(pieces):
        own = part[z, k]
        for side in sides:
            odd_copy(side, 0, k).wait_recv()
            even_copy(side, steps - 1, k).wait_recv()
            own = own + side[1][steps - 1, k] + side[2][0, k]
        for t in range(nx):
            xs[t, k] = own[t * slots : (t + 1) * slots]
        for d in range(1, nx):
            to = at_x(d)
            send(remote(xs.at[to, k], xin.at[x, k], xe_s.at[d, k], xe_r.at[d, k], {"x": to}))
    xin[x] = xs[x]

    tab_in.wait()
    lengths = [lens[asg[w_own * slots + j]] for j in range(slots)]
    angles = jnp.concatenate([tab[pl.ds(lengths[j], 1), :] for j in range(slots)], axis=0)
    turned = pltpu.roll(angles, HD // 2, 1)
    lane = lax.broadcasted_iota(jnp.int32, (slots, HD), 1)
    cosine = jnp.where(lane < HD // 2, angles, turned)
    sine = jnp.where(lane < HD // 2, -turned, angles)

    def rotate(v):
        return (v * cosine + pltpu.roll(v, HD // 2, 1) * sine).astype(BF16).astype(F32)

    for k in range(pieces):
        for d in range(1, nx):
            src = at_x(nx - d)
            remote(xs.at[0, k], xin.at[src, k], xe_s.at[d, k], xe_r.at[d, k], {"x": src}).wait_recv()
    for k in range(nx):
        for i in range(heads_x):
            turned_query = rotate(xin[k, i])
            for j in range(slots):
                q_ref[j, k * heads_x + i : k * heads_x + i + 1, :] = turned_query[j : j + 1]
    keys_new = rotate(xin[0, pieces - 1] + xin[1, pieces - 1])
    values_new = (xin[2, pieces - 1] + xin[3, pieces - 1]).astype(BF16).astype(F32)

    scale = 1.0 / math.sqrt(HD)
    position = lax.broadcasted_iota(jnp.int32, (heads, most), 1)
    for j in range(slots):
        query = q_ref[j]
        own_score = jnp.sum(query * keys_new[j : j + 1], axis=1, keepdims=True) * scale
        scores = dot_t(query.astype(BF16), kc[j]) * scale
        scores = jnp.where(position < lengths[j], scores, -jnp.inf)
        top = jnp.maximum(jnp.max(scores, axis=1, keepdims=True), own_score)
        weights = jnp.exp(scores - top)
        own_weight = jnp.exp(own_score - top)
        totals = jnp.sum(weights, axis=1, keepdims=True) + own_weight
        probs = (weights / totals).astype(BF16)
        own_prob = (own_weight / totals).astype(BF16).astype(F32)
        attended = dot(probs, vc[j]) + own_prob * values_new[j : j + 1]
        for h in range(heads):
            ab[j : j + 1, h * HD : (h + 1) * HD] = attended[h : h + 1]
    ag[w_own] = ab[...].astype(BF16)

    for d in reversed(by_distance(nz)):
        send(remote(ag.at[w_own], ag.at[w_own], az_s.at[d], az_r.at[d], {"z": at_z(d)}))
    for d in [0] + by_distance(nz):
        src_z = at_z(nz - d)
        block = x * nz + src_z
        if d > 0:
            remote(ag.at[block], ag.at[block], az_s.at[d], az_r.at[d], {"z": src_z}).wait_recv()
        for e in range(1, nx):
            send(remote(ag.at[block], ag.at[block], ax_s.at[d, e], ax_r.at[d, e], {"x": at_x(e)}))
    wo_in.wait()
    for d in [0] + by_distance(nz):
        for e in range(1, nx):
            src_x = at_x(nx - e)
            block = src_x * nz + at_z(nz - d)
            remote(ag.at[block], ag.at[block], ax_s.at[d, e], ax_r.at[d, e], {"x": src_x}).wait_recv()

    group = 16 // slots
    for g in range(rows // 16):
        blocks = [ag[g * group + i].astype(F32) for i in range(group)]
        att[g * 16 : (g + 1) * 16, :] = jnp.concatenate(blocks, axis=0).astype(BF16)
    tile = 512
    update = jnp.zeros((rows, wo.shape[1]), F32)
    for k in range(att.shape[1] // tile):
        picked = dot(pr[...], att[:, k * tile : (k + 1) * tile]).astype(BF16)
        update = update + dot(picked, wo[k * tile : (k + 1) * tile, :])
    nst[...] = update.reshape(nn, rows_n, wo.shape[1])
    for d in range(1, nn):
        send(remote(nst.at[at_n(d)], nin.at[n], no_s.at[d], no_r.at[d], {"narrow": at_n(d)}))
    nin[n] = nst[n]
    for d in range(1, nn):
        src = at_n(nn - d)
        remote(nst.at[0], nin.at[src], no_s.at[d], no_r.at[d], {"narrow": src}).wait_recv()
    result = nin[0]
    for k in range(1, nn):
        result = result + nin[k]
    out_ref[...] = (nres[n, x].astype(F32) + result).astype(BF16)

    for copy in sends:
        copy.wait_send()

    @pl.when(x != 0)
    def _():
        k_copy.wait_send()

    @pl.when(x != nx - 1)
    def _():
        v_copy.wait_send()


def per_device(nx, nz, nn, table, residual, norm_gain, w_query, w_keyval, w_out, cache_rows, lengths, assignment):
    slots, most, _, channels = cache_rows.shape
    kw, query_cols = w_query.shape
    rows_n = residual.shape[0]
    rows = rows_n * nn
    qcols = query_cols // nx
    pieces = qcols // HD + 1
    heads = query_cols // HD
    steps = nz // 4
    width = kw * nx * nz
    anywhere = pl.BlockSpec(memory_space=pl.ANY)
    vmem = pl.BlockSpec(memory_space=pltpu.VMEM)
    smem = pl.BlockSpec(memory_space=pltpu.SMEM)
    dma = pltpu.SemaphoreType.DMA
    scratch = [
        pltpu.VMEM((nn, nx, rows_n, kw), BF16),
        pltpu.VMEM((nx, 1, kw), F32),
        pltpu.VMEM((nx, kw, qcols), BF16),
        pltpu.VMEM((2 * kw, HD), BF16),
        pltpu.VMEM((2, kw, HD), BF16),
        pltpu.VMEM((2, kw, HD), BF16),
        pltpu.VMEM(w_out.shape, BF16),
        pltpu.VMEM((slots * most * 2, HD), BF16),
        pltpu.VMEM((slots, most, HD), BF16),
        pltpu.VMEM((slots, most, HD), BF16),
        pltpu.VMEM(table.shape, F32),
        pltpu.VMEM((kw,), BF16),
        pltpu.VMEM((nz, 1, rows), F32),
        pltpu.VMEM((nn, 1, rows), F32),
        pltpu.VMEM((rows, rows), BF16),
        pltpu.VMEM((rows, rows), BF16),
        pltpu.VMEM((rows, nx * kw), BF16),
        pltpu.VMEM((rows, nx * kw), BF16),
        pltpu.VMEM((nz, pieces, nx * slots, HD), F32),
        pltpu.VMEM((steps, pieces, nx * slots, HD), F32),
        pltpu.VMEM((steps, pieces, nx * slots, HD), F32),
        pltpu.VMEM((steps, pieces, nx * slots, HD), F32),
        pltpu.VMEM((steps, pieces, nx * slots, HD), F32),
        pltpu.VMEM((2, kw // 2, qcols), BF16),
        pltpu.VMEM((nx, pieces, slots, HD), F32),
        pltpu.VMEM((nx, pieces, slots, HD), F32),
        pltpu.VMEM((slots, heads, HD), F32),
        pltpu.VMEM((slots, query_cols), F32),
        pltpu.VMEM((nx * nz, slots, query_cols), BF16),
        pltpu.VMEM((rows, query_cols), BF16),
        pltpu.VMEM((nn, rows_n, w_out.shape[1]), F32),
        pltpu.VMEM((nn, rows_n, w_out.shape[1]), F32),
        dma((7,)),
        dma((nx,)), dma((nx,)), dma((nx,)), dma((nx,)), dma((nx,)), dma((nx,)),
        dma((2,)), dma((2,)),
        dma((7,)), dma((7,)),
        dma((nz,)), dma((nz,)),
        dma((nn,)), dma((nn,)),
        *[dma((steps, pieces))] * 8,
        dma((2,)), dma((2,)), dma((2,)), dma((2,)),
        dma((nx, pieces)), dma((nx, pieces)),
        dma((nz,)), dma((nz,)), dma((nz, nx)), dma((nz, nx)),
        dma((nn,)), dma((nn,)),
    ]
    return pl.pallas_call(
        functools.partial(kernel, nx, nz, nn, width),
        out_shape=jax.ShapeDtypeStruct(residual.shape, BF16),
        in_specs=[smem, smem, anywhere, anywhere, vmem] + [anywhere] * 5,
        out_specs=vmem,
        scratch_shapes=scratch,
        compiler_params=pltpu.CompilerParams(
            collective_id=0, has_side_effects=True, vmem_limit_bytes=60 * 1024 * 1024
        ),
        name="decode_block",
    )(
        lengths,
        assignment,
        residual,
        norm_gain,
        assignment.reshape(1, -1),
        w_query,
        w_keyval.reshape(2 * kw, channels),
        w_out,
        cache_rows.reshape(slots * most * 2, channels),
        table,
    )


def solution(mesh):
    nx, nn = 4, mesh.shape["narrow"]
    nz = mesh.shape["wide"] // nx
    torus = Mesh(mesh.devices.reshape(nx, nz, nn), ("x", "z", "narrow"))
    wide = ("x", "z")

    def run(residual, norm_gain, w_query, w_keyval, w_out, cache_rows, lengths, assignment):
        table = jnp.asarray(rotation_table(cache_rows.shape[1]))
        body = jax.shard_map(
            lambda table, *args: per_device(nx, nz, nn, table, *args),
            mesh=torus,
            in_specs=(
                P(),
                P("narrow", wide),
                P(wide),
                P(wide, "narrow"),
                P(wide, None, "narrow"),
                P("narrow", wide),
                P(wide, None, None, "narrow"),
                P(),
                P(),
            ),
            out_specs=P("narrow", wide),
            check_vma=False,
        )
        return body(table, residual, norm_gain, w_query, w_keyval, w_out, cache_rows, lengths, assignment)

    return run
```

```python
import functools
import math

import jax
import jax.numpy as jnp
import numpy as np
from jax import lax
from jax.experimental import pallas as pl
from jax.experimental.pallas import tpu as pltpu
from jax.sharding import Mesh
from jax.sharding import PartitionSpec as P

HD = 128
MESH = pl.DeviceIdType.MESH
F32 = jnp.float32
BF16 = jnp.bfloat16


def rotation_table(most):
    half = HD // 2
    exponents = -(np.arange(half, dtype=np.float32) * np.float32(2.0) / np.float32(HD))
    freqs = np.power(np.float32(500000.0), exponents).astype(np.float32)
    rows = (most + 8) // 8 * 8
    angles = (np.arange(rows, dtype=np.float32)[:, None] * freqs[None, :]).astype(np.float32)
    angles = angles.astype(np.float64)
    return np.concatenate([np.cos(angles), np.sin(angles)], axis=1).astype(np.float32)


def dot(a, b):
    return lax.dot_general(a, b, (((1,), (0,)), ((), ())), preferred_element_type=F32)


def dot_t(a, b):
    return lax.dot_general(a, b, (((1,), (1,)), ((), ())), preferred_element_type=F32)


def by_distance(count):
    return sorted(range(1, count), key=lambda d: min(d, count - d))


def kernel(
    nx, nz, nn, width,
    lens, asg, res_h, gain_h, asg_ref, wq_h, wkv_h, wo_h, cache_h, tab_h,
    out_ref,
    nres, gains, wq, wkv, kvs, kvw, wo, cache, kc, vc, tab,
    gain_v, zin, nsq, pz, pr, sres, nrm, part, r_even, r_odd, l_even, l_odd, wrel, xs, xin, q_ref, ab, ag, att, mine, nst, nin,
    loc, xr_s, xr_r, xg_s, xg_r, xw_s, xw_r, kv_s, kv_r, ng_s, ng_r,
    zs_s, zs_r, ns_s, ns_r, re_s, re_r, ro_s, ro_r, le_s, le_r, lo_s, lo_r, wr_s, wr_r, wf_s, wf_r, xe_s, xe_r,
    az_s, az_r, ax_s, ax_r, no_s, no_r,
):
    x, z, n = lax.axis_index("x"), lax.axis_index("z"), lax.axis_index("narrow")
    y, c = n // 2, n % 2
    ny = nn // 2
    turn = 1 - 2 * c
    rows = pz.shape[0]
    rows_n = rows // nn
    slots = xs.shape[2]
    per_z = nx * slots
    pieces = part.shape[1]
    qcols = wq.shape[2]
    kw = wq.shape[1]
    most = kc.shape[1]
    heads = q_ref.shape[1]
    heads_x = heads // nx
    w_own = x * nz + z

    def remote(src, dst, ss, rs, dev):
        return pltpu.make_async_remote_copy(
            src_ref=src, dst_ref=dst, send_sem=ss, recv_sem=rs, device_id=dev, device_id_type=MESH
        )

    def at_x(d):
        return lax.rem(x + d, nx)

    def at_z(d):
        return lax.rem(z + d, nz)

    def at_n(d):
        return lax.rem(n + d, nn)

    def wq_part(t):
        return wq_h.at[:, pl.ds(pl.multiple_of(t * qcols, qcols), qcols)]

    local = [
        pltpu.make_async_copy(gain_h, gain_v, loc.at[6]),
        pltpu.make_async_copy(wkv_h, wkv, loc.at[0]),
        pltpu.make_async_copy(res_h, nres.at[n, x], loc.at[1]),
        pltpu.make_async_copy(wq_part(x), wq.at[x], loc.at[2]),
        pltpu.make_async_copy(cache_h, cache, loc.at[3]),
        pltpu.make_async_copy(wo_h, wo, loc.at[4]),
        pltpu.make_async_copy(tab_h, tab, loc.at[5]),
    ]
    barrier = pltpu.get_barrier_semaphore()
    for d in reversed(by_distance(nz)):
        pl.semaphore_signal(barrier, inc=1, device_id={"z": at_z(d)}, device_id_type=MESH)
    for d in range(1, nx):
        pl.semaphore_signal(barrier, inc=1, device_id={"x": at_x(d)}, device_id_type=MESH)
    for d in range(1, nn):
        pl.semaphore_signal(barrier, inc=1, device_id={"narrow": at_n(d)}, device_id_type=MESH)
    for copy in local:
        copy.start()
    gain_in, wkv_in, res_in, wq_in, cache_in, wo_in, tab_in = local
    pl.semaphore_wait(barrier, (nx - 1) + (nz - 1) + (nn - 1))

    sends = []

    def send(copy):
        copy.start()
        sends.append(copy)

    def relay_half(i, src, to):
        return remote(src, wrel.at[i], wr_s.at[i], wr_r.at[i], {"x": to})

    def relayed(i, owner, to):
        half = wq.at[owner, i * (kw // 2) : (i + 1) * (kw // 2)]
        return remote(wrel.at[i], half, wf_s.at[i], wf_r.at[i], {"x": to})

    for d in range(1, nx):
        send(remote(res_h, nres.at[n, x], xr_s.at[d], xr_r.at[d], {"x": at_x(d)}))
    gain_in.wait()
    gains[x] = gain_v[...].astype(F32).reshape(1, kw)
    for d in range(1, nx):
        send(remote(gains.at[x], gains.at[x], xg_s.at[d], xg_r.at[d], {"x": at_x(d)}))
    far_cols = pl.ds(pl.multiple_of(at_x(2) * qcols, qcols), qcols)
    send(relay_half(0, wq_h.at[0 : kw // 2, far_cols], at_x(1)))
    send(relay_half(1, wq_h.at[kw // 2 : kw, far_cols], at_x(nx - 1)))
    for d in (1, nx - 1):
        send(remote(wq_part(at_x(d)), wq.at[x], xw_s.at[d], xw_r.at[d], {"x": at_x(d)}))

    a_row = asg_ref[...]
    i_sub = lax.broadcasted_iota(jnp.int32, (rows, rows), 0)
    i_lane = lax.broadcasted_iota(jnp.int32, (rows, rows), 1)
    zz, rest = i_sub // per_z, i_sub % per_z
    slot_of = ((rest // slots) * nz + zz) * slots + rest % slots
    a_col = jnp.sum(
        jnp.where(i_lane == slot_of, a_row.astype(F32), 0.0), axis=1, keepdims=True
    ).astype(jnp.int32)
    pick = i_lane == a_col
    pz[...] = jnp.where(pick, 1.0, 0.0).astype(BF16)
    pr[...] = jnp.where(i_sub == a_row, 1.0, 0.0).astype(BF16)

    e_row = lax.broadcasted_iota(jnp.int32, (kw, 2 * kw), 0)
    e_col = lax.broadcasted_iota(jnp.int32, (kw, 2 * kw), 1)
    e0 = jnp.where(e_col == 2 * e_row, 1.0, 0.0).astype(BF16)
    e1 = jnp.where(e_col == 2 * e_row + 1, 1.0, 0.0).astype(BF16)
    wkv_in.wait()
    kvs[0] = dot(e0, wkv[...]).astype(BF16)
    kvs[1] = dot(e1, wkv[...]).astype(BF16)

    kv_slot = lax.rem(x, 2)
    k_copy = remote(kvs.at[0], kvw.at[kv_slot], kv_s.at[0], kv_r.at[kv_slot], {"x": x // 2})
    v_copy = remote(kvs.at[1], kvw.at[kv_slot], kv_s.at[1], kv_r.at[kv_slot], {"x": 2 + x // 2})

    @pl.when(x != 0)
    def _():
        k_copy.start()

    @pl.when(x == 0)
    def _():
        kvw[0] = kvs[0]

    @pl.when(x != nx - 1)
    def _():
        v_copy.start()

    @pl.when(x == nx - 1)
    def _():
        kvw[1] = kvs[1]

    def narrow(dy, core):
        return lax.rem(y + dy + ny, ny) * 2 + core

    def row_copy(k, src, to):
        return remote(nres.at[src], nres.at[src], ng_s.at[k], ng_r.at[k], {"narrow": to})

    res_in.wait()
    for d in range(1, nx):
        src = at_x(nx - d)
        remote(res_h, nres.at[n, src], xr_s.at[d], xr_r.at[d], {"x": src}).wait_recv()
    ahead, behind, across = narrow(turn, c), narrow(-turn, c), narrow(2, c)
    other = narrow(0, 1 - c)
    send(row_copy(0, n, ahead))
    send(row_copy(1, n, behind))
    send(row_copy(3, n, other))

    squares = jnp.zeros((rows_n, 1), F32)
    for k in range(nx):
        block = nres[n, k].astype(F32)
        squares = squares + jnp.sum(block * block, axis=1, keepdims=True)
    r_sub = lax.broadcasted_iota(jnp.int32, (rows_n, rows), 0)
    r_lane = lax.broadcasted_iota(jnp.int32, (rows_n, rows), 1)
    zin[z] = jnp.sum(jnp.where(r_lane == r_sub + n * rows_n, squares, 0.0), axis=0, keepdims=True)
    for d in reversed(by_distance(nz)):
        send(remote(zin.at[z], zin.at[z], zs_s.at[d], zs_r.at[d], {"z": at_z(d)}))

    cache_in.wait()
    step = kw
    for j in range(slots):
        for b in range(most // step):
            block = cache[pl.ds((j * most + b * step) * 2, 2 * step), :]
            kc[j, b * step : (b + 1) * step, :] = dot(e0, block).astype(BF16)
            vc[j, b * step : (b + 1) * step, :] = dot(e1, block).astype(BF16)

    left_x, right_x, opposite = at_x(nx - 1), at_x(1), at_x(2)
    relay_half(0, wrel.at[0], left_x).wait_recv()
    send(relayed(0, left_x, right_x))
    relay_half(1, wrel.at[1], right_x).wait_recv()
    send(relayed(1, right_x, left_x))

    row_copy(0, behind, behind).wait_recv()
    send(row_copy(2, behind, ahead))
    send(row_copy(4, behind, other))
    row_copy(1, ahead, ahead).wait_recv()
    send(row_copy(5, ahead, other))
    row_copy(2, across, behind).wait_recv()
    send(row_copy(6, across, other))

    for d in range(1, nz):
        src = at_z(nz - d)
        remote(zin.at[src], zin.at[src], zs_s.at[d], zs_r.at[d], {"z": src}).wait_recv()
    nsq[n] = jnp.sum(zin[...], axis=0)
    for d in range(1, nn):
        send(remote(nsq.at[n], nsq.at[n], ns_s.at[d], ns_r.at[d], {"narrow": at_n(d)}))

    far = narrow(-2 * turn, 1 - c)
    for k, src in ((3, other), (4, narrow(turn, 1 - c)), (5, narrow(-turn, 1 - c)), (6, far)):
        row_copy(k, src, other).wait_recv()
    for k in range(nx):
        block = nres[:, k].reshape(rows, kw)
        sres[:, k * kw : (k + 1) * kw] = dot(pz[...], block).astype(BF16)

    for d in range(1, nn):
        src = at_n(nn - d)
        remote(nsq.at[src], nsq.at[src], ns_s.at[d], ns_r.at[d], {"narrow": src}).wait_recv()
    sums = jnp.sum(nsq[...], axis=0)
    sum_col = jnp.sum(jnp.where(pz[...].astype(F32) > 0.5, sums, 0.0), axis=1, keepdims=True)
    inverse = lax.rsqrt(sum_col / width + 1e-05)

    for d in range(1, nx):
        src = at_x(nx - d)
        remote(gains.at[src], gains.at[src], xg_s.at[d], xg_r.at[d], {"x": src}).wait_recv()
    for k in range(nx):
        block = sres[:, k * kw : (k + 1) * kw].astype(F32)
        nrm[:, k * kw : (k + 1) * kw] = (block * inverse * gains[k]).astype(BF16)

    wq_in.wait()
    for d in (1, nx - 1):
        src = at_x(nx - d)
        remote(wq_part(src), wq.at[src], xw_s.at[d], xw_r.at[d], {"x": src}).wait_recv()
    relayed(0, opposite, left_x).wait_recv()
    relayed(1, opposite, right_x).wait_recv()

    @pl.when(x != 0)
    def _():
        remote(kvs.at[0], kvw.at[0], kv_s.at[0], kv_r.at[0], {"x": x // 2}).wait_recv()

    @pl.when(x != nx - 1)
    def _():
        remote(kvs.at[0], kvw.at[1], kv_s.at[0], kv_r.at[1], {"x": x // 2}).wait_recv()

    total = dot(nrm[:, :kw], wq[0])
    for k in range(1, nx):
        total = total + dot(nrm[:, k * kw : (k + 1) * kw], wq[k])
    for k in range(pieces - 1):
        part[:, k] = total[:, k * HD : (k + 1) * HD].reshape(nz, per_z, HD)
    half = nrm[:, pl.ds(pl.multiple_of(lax.rem(x, 2) * 2 * kw, 2 * kw), 2 * kw)]
    kv_part = dot(half[:, :kw], kvw[0]) + dot(half[:, kw:], kvw[1])
    part[:, pieces - 1] = kv_part.reshape(nz, per_z, HD)

    steps = nz // 4
    sides = ((1, r_even, r_odd, re_s, re_r, ro_s, ro_r), (-1, l_even, l_odd, le_s, le_r, lo_s, lo_r))

    def along(side, d):
        return at_z(d if side[0] > 0 else nz - d)

    def odd_copy(side, i, k):
        src = part.at[along(side, 2 * i + 1), k]
        to = {"z": along(side, 1)}
        return remote(src, side[2].at[i, k], side[5].at[i, k], side[6].at[i, k], to)

    def even_copy(side, s, k):
        if s == 0:
            src = part.at[along(side, 2 * steps), k]
        elif s == 1 and side[0] < 0:
            src = side[2].at[steps - 1, k]
        else:
            src = side[1].at[s - 1, k]
        to = {"z": along(side, 2)}
        return remote(src, side[1].at[s, k], side[3].at[s, k], side[4].at[s, k], to)

    for k in range(pieces):
        send(even_copy(sides[0], 0, k))
        for side in sides:
            send(odd_copy(side, steps - 1, k))
    for i in range(steps - 2, -1, -1):
        for k in range(pieces):
            for side in sides:
                send(odd_copy(side, i, k))
    for s in range(1, steps):
        for k in range(pieces):
            for side in sides:
                own_part = part[along(side, 2 * (steps - s)), k]
                odd_copy(side, steps - s, k).wait_recv()
                if s == 1 and side[0] < 0:
                    side[2][steps - 1, k] = side[2][steps - 1, k] + own_part
                else:
                    even_copy(side, s - 1, k).wait_recv()
                    side[1][s - 1, k] = side[1][s - 1, k] + side[2][steps - s, k] + own_part
                send(even_copy(side, s, k))
    for k in range(pieces):
        own = part[z, k]
        for side in sides:
            odd_copy(side, 0, k).wait_recv()
            even_copy(side, steps - 1, k).wait_recv()
            own = own + side[1][steps - 1, k] + side[2][0, k]
        for t in range(nx):
            xs[t, k] = own[t * slots : (t + 1) * slots]
        for d in range(1, nx):
            to = at_x(d)
            send(remote(xs.at[to, k], xin.at[x, k], xe_s.at[d, k], xe_r.at[d, k], {"x": to}))
    xin[x] = xs[x]

    tab_in.wait()
    lengths = [lens[asg[w_own * slots + j]] for j in range(slots)]
    angles = jnp.concatenate([tab[pl.ds(lengths[j], 1), :] for j in range(slots)], axis=0)
    turned = pltpu.roll(angles, HD // 2, 1)
    lane = lax.broadcasted_iota(jnp.int32, (slots, HD), 1)
    cosine = jnp.where(lane < HD // 2, angles, turned)
    sine = jnp.where(lane < HD // 2, -turned, angles)

    def rotate(v):
        return (v * cosine + pltpu.roll(v, HD // 2, 1) * sine).astype(BF16).astype(F32)

    for k in range(pieces):
        for d in range(1, nx):
            src = at_x(nx - d)
            remote(xs.at[0, k], xin.at[src, k], xe_s.at[d, k], xe_r.at[d, k], {"x": src}).wait_recv()
    for k in range(nx):
        for i in range(heads_x):
            turned_query = rotate(xin[k, i])
            for j in range(slots):
                q_ref[j, k * heads_x + i : k * heads_x + i + 1, :] = turned_query[j : j + 1]
    keys_new = rotate(xin[0, pieces - 1] + xin[1, pieces - 1])
    values_new = (xin[2, pieces - 1] + xin[3, pieces - 1]).astype(BF16).astype(F32)

    scale = 1.0 / math.sqrt(HD)
    position = lax.broadcasted_iota(jnp.int32, (heads, most), 1)
    for j in range(slots):
        query = q_ref[j]
        own_score = jnp.sum(query * keys_new[j : j + 1], axis=1, keepdims=True) * scale
        scores = dot_t(query.astype(BF16), kc[j]) * scale
        scores = jnp.where(position < lengths[j], scores, -jnp.inf)
        top = jnp.maximum(jnp.max(scores, axis=1, keepdims=True), own_score)
        weights = jnp.exp(scores - top)
        own_weight = jnp.exp(own_score - top)
        totals = jnp.sum(weights, axis=1, keepdims=True) + own_weight
        probs = (weights / totals).astype(BF16)
        own_prob = (own_weight / totals).astype(BF16).astype(F32)
        attended = dot(probs, vc[j]) + own_prob * values_new[j : j + 1]
        for h in range(heads):
            ab[j : j + 1, h * HD : (h + 1) * HD] = attended[h : h + 1]
    ag[w_own] = ab[...].astype(BF16)

    reach = nz // 4

    def z_copy(d, block, to):
        return remote(ag.at[block], ag.at[block], az_s.at[d], az_r.at[d], {"z": to})

    def x_copy(d, e, block, to):
        return remote(ag.at[block], ag.at[block], ax_s.at[d, e], ax_r.at[d, e], {"x": to})

    def block_of(e, d):
        return at_x(nx - e) * nz + at_z(nz - d)

    def along_x(d, hops):
        for e in hops:
            send(x_copy(d, e, block_of(0, d), at_x(e)))

    for k in range(reach, 0, -1):
        send(z_copy(k, w_own, at_z(k)))
        send(z_copy(nz - k, w_own, at_z(nz - k)))
    order = [0] + by_distance(nz)
    near = [d for d in order if min(d, nz - d) <= reach]
    far = [d for d in order if min(d, nz - d) > reach]
    along_x(0, (1, nx - 1))
    for d in (reach, nz - reach):
        z_copy(d, block_of(0, d), z).wait_recv()
        if d == reach:
            for k in range(reach, 0, -1):
                send(z_copy(reach + k, block_of(0, d), at_z(k)))
        else:
            for k in range(reach - 1, 0, -1):
                send(z_copy(nz - reach - k, block_of(0, d), at_z(nz - k)))
    for d in near[1:]:
        if d not in (reach, nz - reach):
            z_copy(d, block_of(0, d), z).wait_recv()
        along_x(d, (1, nx - 1))
    for d in near:
        e = 1 if d % 2 == 0 else nx - 1
        x_copy(d, e, block_of(e, d), x).wait_recv()
        send(x_copy(d, 2, block_of(e, d), at_x(e)))
    for d in far:
        z_copy(d, block_of(0, d), z).wait_recv()
        along_x(d, (1, nx - 1, 2))
    wo_in.wait()
    for d in order:
        passed = 1 if d % 2 == 0 else nx - 1
        for e in range(1, nx):
            if d in far or e != passed:
                x_copy(d, e, block_of(e, d), x).wait_recv()

    group = 16 // slots
    for g in range(rows // 16):
        blocks = [ag[g * group + i].astype(F32) for i in range(group)]
        att[g * 16 : (g + 1) * 16, :] = jnp.concatenate(blocks, axis=0).astype(BF16)
    tile = 512
    update = jnp.zeros((rows, wo.shape[1]), F32)
    for k in range(att.shape[1] // tile):
        picked = dot(pr[...], att[:, k * tile : (k + 1) * tile]).astype(BF16)
        update = update + dot(picked, wo[k * tile : (k + 1) * tile, :])
    total = update.reshape(nn, rows_n, wo.shape[1])
    mine[...] = total
    nst[...] = total.astype(BF16)
    for d in range(1, nn):
        send(remote(nst.at[at_n(d)], nin.at[d], no_s.at[d], no_r.at[d], {"narrow": at_n(d)}))
    result = mine[n]
    for d in range(1, nn):
        src = at_n(nn - d)
        remote(nst.at[0], nin.at[d], no_s.at[d], no_r.at[d], {"narrow": src}).wait_recv()
        result = result + nin[d].astype(F32)
    out_ref[...] = (nres[n, x].astype(F32) + result).astype(BF16)

    for copy in sends:
        copy.wait_send()

    @pl.when(x != 0)
    def _():
        k_copy.wait_send()

    @pl.when(x != nx - 1)
    def _():
        v_copy.wait_send()


def per_device(nx, nz, nn, table, residual, norm_gain, w_query, w_keyval, w_out, cache_rows, lengths, assignment):
    slots, most, _, channels = cache_rows.shape
    kw, query_cols = w_query.shape
    rows_n = residual.shape[0]
    rows = rows_n * nn
    qcols = query_cols // nx
    pieces = qcols // HD + 1
    heads = query_cols // HD
    steps = nz // 4
    width = kw * nx * nz
    anywhere = pl.BlockSpec(memory_space=pl.ANY)
    vmem = pl.BlockSpec(memory_space=pltpu.VMEM)
    smem = pl.BlockSpec(memory_space=pltpu.SMEM)
    dma = pltpu.SemaphoreType.DMA
    scratch = [
        pltpu.VMEM((nn, nx, rows_n, kw), BF16),
        pltpu.VMEM((nx, 1, kw), F32),
        pltpu.VMEM((nx, kw, qcols), BF16),
        pltpu.VMEM((2 * kw, HD), BF16),
        pltpu.VMEM((2, kw, HD), BF16),
        pltpu.VMEM((2, kw, HD), BF16),
        pltpu.VMEM(w_out.shape, BF16),
        pltpu.VMEM((slots * most * 2, HD), BF16),
        pltpu.VMEM((slots, most, HD), BF16),
        pltpu.VMEM((slots, most, HD), BF16),
        pltpu.VMEM(table.shape, F32),
        pltpu.VMEM((kw,), BF16),
        pltpu.VMEM((nz, 1, rows), F32),
        pltpu.VMEM((nn, 1, rows), F32),
        pltpu.VMEM((rows, rows), BF16),
        pltpu.VMEM((rows, rows), BF16),
        pltpu.VMEM((rows, nx * kw), BF16),
        pltpu.VMEM((rows, nx * kw), BF16),
        pltpu.VMEM((nz, pieces, nx * slots, HD), F32),
        pltpu.VMEM((steps, pieces, nx * slots, HD), F32),
        pltpu.VMEM((steps, pieces, nx * slots, HD), F32),
        pltpu.VMEM((steps, pieces, nx * slots, HD), F32),
        pltpu.VMEM((steps, pieces, nx * slots, HD), F32),
        pltpu.VMEM((2, kw // 2, qcols), BF16),
        pltpu.VMEM((nx, pieces, slots, HD), F32),
        pltpu.VMEM((nx, pieces, slots, HD), F32),
        pltpu.VMEM((slots, heads, HD), F32),
        pltpu.VMEM((slots, query_cols), F32),
        pltpu.VMEM((nx * nz, slots, query_cols), BF16),
        pltpu.VMEM((rows, query_cols), BF16),
        pltpu.VMEM((nn, rows_n, w_out.shape[1]), F32),
        pltpu.VMEM((nn, rows_n, w_out.shape[1]), BF16),
        pltpu.VMEM((nn, rows_n, w_out.shape[1]), BF16),
        dma((7,)),
        dma((nx,)), dma((nx,)), dma((nx,)), dma((nx,)), dma((nx,)), dma((nx,)),
        dma((2,)), dma((2,)),
        dma((7,)), dma((7,)),
        dma((nz,)), dma((nz,)),
        dma((nn,)), dma((nn,)),
        *[dma((steps, pieces))] * 8,
        dma((2,)), dma((2,)), dma((2,)), dma((2,)),
        dma((nx, pieces)), dma((nx, pieces)),
        dma((nz,)), dma((nz,)), dma((nz, nx)), dma((nz, nx)),
        dma((nn,)), dma((nn,)),
    ]
    return pl.pallas_call(
        functools.partial(kernel, nx, nz, nn, width),
        out_shape=jax.ShapeDtypeStruct(residual.shape, BF16),
        in_specs=[smem, smem, anywhere, anywhere, vmem] + [anywhere] * 5,
        out_specs=vmem,
        scratch_shapes=scratch,
        compiler_params=pltpu.CompilerParams(
            collective_id=0, has_side_effects=True, vmem_limit_bytes=60 * 1024 * 1024
        ),
        name="decode_block",
    )(
        lengths,
        assignment,
        residual,
        norm_gain,
        assignment.reshape(1, -1),
        w_query,
        w_keyval.reshape(2 * kw, channels),
        w_out,
        cache_rows.reshape(slots * most * 2, channels),
        table,
    )


def solution(mesh):
    nx, nn = 4, mesh.shape["narrow"]
    nz = mesh.shape["wide"] // nx
    torus = Mesh(mesh.devices.reshape(nx, nz, nn), ("x", "z", "narrow"))
    wide = ("x", "z")

    def run(residual, norm_gain, w_query, w_keyval, w_out, cache_rows, lengths, assignment):
        table = jnp.asarray(rotation_table(cache_rows.shape[1]))
        body = jax.shard_map(
            lambda table, *args: per_device(nx, nz, nn, table, *args),
            mesh=torus,
            in_specs=(
                P(),
                P("narrow", wide),
                P(wide),
                P(wide, "narrow"),
                P(wide, None, "narrow"),
                P("narrow", wide),
                P(wide, None, None, "narrow"),
                P(),
                P(),
            ),
            out_specs=P("narrow", wide),
            check_vma=False,
        )
        return body(table, residual, norm_gain, w_query, w_keyval, w_out, cache_rows, lengths, assignment)

    return run
```

```python
import functools
import math

import jax
import jax.numpy as jnp
import numpy as np
from jax import lax
from jax.experimental import pallas as pl
from jax.experimental.pallas import tpu as pltpu
from jax.sharding import Mesh
from jax.sharding import PartitionSpec as P

HD = 128
MESH = pl.DeviceIdType.MESH
F32 = jnp.float32
BF16 = jnp.bfloat16


def rotation_table(most):
    half = HD // 2
    exponents = -(np.arange(half, dtype=np.float32) * np.float32(2.0) / np.float32(HD))
    freqs = np.power(np.float32(500000.0), exponents).astype(np.float32)
    rows = (most + 8) // 8 * 8
    angles = (np.arange(rows, dtype=np.float32)[:, None] * freqs[None, :]).astype(np.float32)
    angles = angles.astype(np.float64)
    return np.concatenate([np.cos(angles), np.sin(angles)], axis=1).astype(np.float32)


def dot(a, b):
    return lax.dot_general(a, b, (((1,), (0,)), ((), ())), preferred_element_type=F32)


def dot_t(a, b):
    return lax.dot_general(a, b, (((1,), (1,)), ((), ())), preferred_element_type=F32)


def by_distance(count):
    return sorted(range(1, count), key=lambda d: min(d, count - d))


def kernel(
    nx, nz, nn, width,
    lens, asg, res_h, gain_h, asg_ref, wq_h, wkv_h, wo_h, cache_h, tab_h,
    out_ref,
    nres, gains, wq, wkv, kvs, kvw, wo, cache, kc, vc, tab,
    gain_v, zin, nsq, pz, pr, sres, nrm, part, r_even, r_odd, l_even, l_odd, wrel, xs, xin, q_ref, ab, ag, att, mine, nst, nin,
    loc, xr_s, xr_r, xg_s, xg_r, xw_s, xw_r, kv_s, kv_r, ng_s, ng_r,
    zs_s, zs_r, ns_s, ns_r, re_s, re_r, ro_s, ro_r, le_s, le_r, lo_s, lo_r, wr_s, wr_r, wf_s, wf_r, xe_s, xe_r,
    az_s, az_r, ax_s, ax_r, no_s, no_r,
):
    x, z, n = lax.axis_index("x"), lax.axis_index("z"), lax.axis_index("narrow")
    y, c = n // 2, n % 2
    ny = nn // 2
    turn = 1 - 2 * c
    rows = pz.shape[0]
    rows_n = rows // nn
    slots = xs.shape[2]
    per_z = nx * slots
    pieces = part.shape[1]
    qcols = wq.shape[2]
    kw = wq.shape[1]
    most = kc.shape[1]
    heads = q_ref.shape[1]
    heads_x = heads // nx
    w_own = x * nz + z

    def remote(src, dst, ss, rs, dev):
        return pltpu.make_async_remote_copy(
            src_ref=src, dst_ref=dst, send_sem=ss, recv_sem=rs, device_id=dev, device_id_type=MESH
        )

    def at_x(d):
        return lax.rem(x + d, nx)

    def at_z(d):
        return lax.rem(z + d, nz)

    def at_n(d):
        return lax.rem(n + d, nn)

    def wq_part(t):
        return wq_h.at[:, pl.ds(pl.multiple_of(t * qcols, qcols), qcols)]

    local = [
        pltpu.make_async_copy(gain_h, gain_v, loc.at[6]),
        pltpu.make_async_copy(wkv_h, wkv, loc.at[0]),
        pltpu.make_async_copy(res_h, nres.at[n, x], loc.at[1]),
        pltpu.make_async_copy(wq_part(x), wq.at[x], loc.at[2]),
        pltpu.make_async_copy(cache_h, cache, loc.at[3]),
        pltpu.make_async_copy(wo_h, wo, loc.at[4]),
        pltpu.make_async_copy(tab_h, tab, loc.at[5]),
    ]
    barrier = pltpu.get_barrier_semaphore()
    for d in reversed(by_distance(nz)):
        pl.semaphore_signal(barrier, inc=1, device_id={"z": at_z(d)}, device_id_type=MESH)
    for d in range(1, nx):
        pl.semaphore_signal(barrier, inc=1, device_id={"x": at_x(d)}, device_id_type=MESH)
    for d in range(1, nn):
        pl.semaphore_signal(barrier, inc=1, device_id={"narrow": at_n(d)}, device_id_type=MESH)
    for copy in local:
        copy.start()
    gain_in, wkv_in, res_in, wq_in, cache_in, wo_in, tab_in = local
    pl.semaphore_wait(barrier, (nx - 1) + (nz - 1) + (nn - 1))

    sends = []

    def send(copy):
        copy.start()
        sends.append(copy)

    def relay_half(i, src, to):
        return remote(src, wrel.at[i], wr_s.at[i], wr_r.at[i], {"x": to})

    def relayed(i, owner, to):
        half = wq.at[owner, i * (kw // 2) : (i + 1) * (kw // 2)]
        return remote(wrel.at[i], half, wf_s.at[i], wf_r.at[i], {"x": to})

    for d in range(1, nx):
        send(remote(res_h, nres.at[n, x], xr_s.at[d], xr_r.at[d], {"x": at_x(d)}))
    gain_in.wait()
    gains[x] = gain_v[...].astype(F32).reshape(1, kw)
    for d in range(1, nx):
        send(remote(gains.at[x], gains.at[x], xg_s.at[d], xg_r.at[d], {"x": at_x(d)}))
    far_cols = pl.ds(pl.multiple_of(at_x(2) * qcols, qcols), qcols)
    send(relay_half(0, wq_h.at[0 : kw // 2, far_cols], at_x(1)))
    send(relay_half(1, wq_h.at[kw // 2 : kw, far_cols], at_x(nx - 1)))
    for d in (1, nx - 1):
        send(remote(wq_part(at_x(d)), wq.at[x], xw_s.at[d], xw_r.at[d], {"x": at_x(d)}))

    a_row = asg_ref[...]
    i_sub = lax.broadcasted_iota(jnp.int32, (rows, rows), 0)
    i_lane = lax.broadcasted_iota(jnp.int32, (rows, rows), 1)
    zz, rest = i_sub // per_z, i_sub % per_z
    slot_of = ((rest // slots) * nz + zz) * slots + rest % slots
    a_col = jnp.sum(
        jnp.where(i_lane == slot_of, a_row.astype(F32), 0.0), axis=1, keepdims=True
    ).astype(jnp.int32)
    pick = i_lane == a_col
    pz[...] = jnp.where(pick, 1.0, 0.0).astype(BF16)
    pr[...] = jnp.where(i_sub == a_row, 1.0, 0.0).astype(BF16)

    e_row = lax.broadcasted_iota(jnp.int32, (kw, 2 * kw), 0)
    e_col = lax.broadcasted_iota(jnp.int32, (kw, 2 * kw), 1)
    e0 = jnp.where(e_col == 2 * e_row, 1.0, 0.0).astype(BF16)
    e1 = jnp.where(e_col == 2 * e_row + 1, 1.0, 0.0).astype(BF16)
    wkv_in.wait()
    kvs[0] = dot(e0, wkv[...]).astype(BF16)
    kvs[1] = dot(e1, wkv[...]).astype(BF16)

    kv_slot = lax.rem(x, 2)
    k_copy = remote(kvs.at[0], kvw.at[kv_slot], kv_s.at[0], kv_r.at[kv_slot], {"x": x // 2})
    v_copy = remote(kvs.at[1], kvw.at[kv_slot], kv_s.at[1], kv_r.at[kv_slot], {"x": 2 + x // 2})

    @pl.when(x != 0)
    def _():
        k_copy.start()

    @pl.when(x == 0)
    def _():
        kvw[0] = kvs[0]

    @pl.when(x != nx - 1)
    def _():
        v_copy.start()

    @pl.when(x == nx - 1)
    def _():
        kvw[1] = kvs[1]

    def narrow(dy, core):
        return lax.rem(y + dy + ny, ny) * 2 + core

    def row_copy(k, src, to):
        return remote(nres.at[src], nres.at[src], ng_s.at[k], ng_r.at[k], {"narrow": to})

    res_in.wait()
    for d in range(1, nx):
        src = at_x(nx - d)
        remote(res_h, nres.at[n, src], xr_s.at[d], xr_r.at[d], {"x": src}).wait_recv()
    ahead, behind, across = narrow(turn, c), narrow(-turn, c), narrow(2, c)
    other = narrow(0, 1 - c)
    send(row_copy(0, n, ahead))
    send(row_copy(1, n, behind))
    send(row_copy(3, n, other))

    squares = jnp.zeros((rows_n, 1), F32)
    for k in range(nx):
        block = nres[n, k].astype(F32)
        squares = squares + jnp.sum(block * block, axis=1, keepdims=True)
    r_sub = lax.broadcasted_iota(jnp.int32, (rows_n, rows), 0)
    r_lane = lax.broadcasted_iota(jnp.int32, (rows_n, rows), 1)
    zin[z] = jnp.sum(jnp.where(r_lane == r_sub + n * rows_n, squares, 0.0), axis=0, keepdims=True)
    for d in reversed(by_distance(nz)):
        send(remote(zin.at[z], zin.at[z], zs_s.at[d], zs_r.at[d], {"z": at_z(d)}))

    cache_in.wait()
    step = kw
    for j in range(slots):
        for b in range(most // step):
            block = cache[pl.ds((j * most + b * step) * 2, 2 * step), :]
            kc[j, b * step : (b + 1) * step, :] = dot(e0, block).astype(BF16)
            vc[j, b * step : (b + 1) * step, :] = dot(e1, block).astype(BF16)

    left_x, right_x, opposite = at_x(nx - 1), at_x(1), at_x(2)
    relay_half(0, wrel.at[0], left_x).wait_recv()
    send(relayed(0, left_x, right_x))
    relay_half(1, wrel.at[1], right_x).wait_recv()
    send(relayed(1, right_x, left_x))

    row_copy(0, behind, behind).wait_recv()
    send(row_copy(2, behind, ahead))
    send(row_copy(4, behind, other))
    row_copy(1, ahead, ahead).wait_recv()
    send(row_copy(5, ahead, other))
    row_copy(2, across, behind).wait_recv()
    send(row_copy(6, across, other))

    for d in range(1, nz):
        src = at_z(nz - d)
        remote(zin.at[src], zin.at[src], zs_s.at[d], zs_r.at[d], {"z": src}).wait_recv()
    nsq[n] = jnp.sum(zin[...], axis=0)
    for d in range(1, nn):
        send(remote(nsq.at[n], nsq.at[n], ns_s.at[d], ns_r.at[d], {"narrow": at_n(d)}))

    far = narrow(-2 * turn, 1 - c)
    for k, src in ((3, other), (4, narrow(turn, 1 - c)), (5, narrow(-turn, 1 - c)), (6, far)):
        row_copy(k, src, other).wait_recv()
    for k in range(nx):
        block = nres[:, k].reshape(rows, kw)
        sres[:, k * kw : (k + 1) * kw] = dot(pz[...], block).astype(BF16)

    for d in range(1, nn):
        src = at_n(nn - d)
        remote(nsq.at[src], nsq.at[src], ns_s.at[d], ns_r.at[d], {"narrow": src}).wait_recv()
    sums = jnp.sum(nsq[...], axis=0)
    sum_col = jnp.sum(jnp.where(pz[...].astype(F32) > 0.5, sums, 0.0), axis=1, keepdims=True)
    inverse = lax.rsqrt(sum_col / width + 1e-05)

    for d in range(1, nx):
        src = at_x(nx - d)
        remote(gains.at[src], gains.at[src], xg_s.at[d], xg_r.at[d], {"x": src}).wait_recv()
    for k in range(nx):
        block = sres[:, k * kw : (k + 1) * kw].astype(F32)
        nrm[:, k * kw : (k + 1) * kw] = (block * inverse * gains[k]).astype(BF16)

    wq_in.wait()
    for d in (1, nx - 1):
        src = at_x(nx - d)
        remote(wq_part(src), wq.at[src], xw_s.at[d], xw_r.at[d], {"x": src}).wait_recv()
    relayed(0, opposite, left_x).wait_recv()
    relayed(1, opposite, right_x).wait_recv()

    @pl.when(x != 0)
    def _():
        remote(kvs.at[0], kvw.at[0], kv_s.at[0], kv_r.at[0], {"x": x // 2}).wait_recv()

    @pl.when(x != nx - 1)
    def _():
        remote(kvs.at[0], kvw.at[1], kv_s.at[0], kv_r.at[1], {"x": x // 2}).wait_recv()

    steps = nz // 4
    sides = ((1, r_even, r_odd, re_s, re_r, ro_s, ro_r), (-1, l_even, l_odd, le_s, le_r, lo_s, lo_r))

    def along(side, d):
        return at_z(d if side[0] > 0 else nz - d)

    def odd_copy(side, i, k):
        src = part.at[along(side, 2 * i + 1), k]
        to = {"z": along(side, 1)}
        return remote(src, side[2].at[i, k], side[5].at[i, k], side[6].at[i, k], to)

    def even_copy(side, s, k):
        if s == 0:
            src = part.at[along(side, 2 * steps), k]
        elif s == 1 and side[0] < 0:
            src = side[2].at[steps - 1, k]
        else:
            src = side[1].at[s - 1, k]
        to = {"z": along(side, 2)}
        return remote(src, side[1].at[s, k], side[3].at[s, k], side[4].at[s, k], to)

    def start_piece(k):
        send(even_copy(sides[0], 0, k))
        for side in sides:
            send(odd_copy(side, steps - 1, k))

    for k in range(0, pieces - 1, 2):
        cols = slice(k * HD, (k + 2) * HD)
        total = dot(nrm[:, :kw], wq[0, :, cols])
        for t in range(1, nx):
            total = total + dot(nrm[:, t * kw : (t + 1) * kw], wq[t, :, cols])
        for h in range(2):
            part[:, k + h] = total[:, h * HD : (h + 1) * HD].reshape(nz, per_z, HD)
            start_piece(k + h)
    half = nrm[:, pl.ds(pl.multiple_of(lax.rem(x, 2) * 2 * kw, 2 * kw), 2 * kw)]
    kv_part = dot(half[:, :kw], kvw[0]) + dot(half[:, kw:], kvw[1])
    part[:, pieces - 1] = kv_part.reshape(nz, per_z, HD)
    start_piece(pieces - 1)
    for k in range(pieces):
        for side in sides:
            send(odd_copy(side, steps - 2, k))
    for s in range(1, steps):
        for k in range(pieces):
            for side in sides:
                own_part = part[along(side, 2 * (steps - s)), k]
                odd_copy(side, steps - s, k).wait_recv()
                if s == 1 and side[0] < 0:
                    side[2][steps - 1, k] = side[2][steps - 1, k] + own_part
                else:
                    even_copy(side, s - 1, k).wait_recv()
                    side[1][s - 1, k] = side[1][s - 1, k] + side[2][steps - s, k] + own_part
                send(even_copy(side, s, k))
        if s + 1 < steps:
            for k in range(pieces):
                for side in sides:
                    send(odd_copy(side, steps - s - 2, k))
    for k in range(pieces):
        own = part[z, k]
        for side in sides:
            odd_copy(side, 0, k).wait_recv()
            even_copy(side, steps - 1, k).wait_recv()
            own = own + side[1][steps - 1, k] + side[2][0, k]
        for t in range(nx):
            xs[t, k] = own[t * slots : (t + 1) * slots]
        for d in range(1, nx):
            to = at_x(d)
            send(remote(xs.at[to, k], xin.at[x, k], xe_s.at[d, k], xe_r.at[d, k], {"x": to}))
    xin[x] = xs[x]

    tab_in.wait()
    lengths = [lens[asg[w_own * slots + j]] for j in range(slots)]
    angles = jnp.concatenate([tab[pl.ds(lengths[j], 1), :] for j in range(slots)], axis=0)
    turned = pltpu.roll(angles, HD // 2, 1)
    lane = lax.broadcasted_iota(jnp.int32, (slots, HD), 1)
    cosine = jnp.where(lane < HD // 2, angles, turned)
    sine = jnp.where(lane < HD // 2, -turned, angles)

    def rotate(v):
        return (v * cosine + pltpu.roll(v, HD // 2, 1) * sine).astype(BF16).astype(F32)

    for i in range(pieces):
        for d in range(1, nx):
            src = at_x(nx - d)
            remote(xs.at[0, i], xin.at[src, i], xe_s.at[d, i], xe_r.at[d, i], {"x": src}).wait_recv()
        for k in range(nx if i < heads_x else 0):
            turned_query = rotate(xin[k, i])
            for j in range(slots):
                q_ref[j, k * heads_x + i : k * heads_x + i + 1, :] = turned_query[j : j + 1]
    keys_new = rotate(xin[0, pieces - 1] + xin[1, pieces - 1])
    values_new = (xin[2, pieces - 1] + xin[3, pieces - 1]).astype(BF16).astype(F32)

    scale = 1.0 / math.sqrt(HD)
    position = lax.broadcasted_iota(jnp.int32, (heads, most), 1)
    for j in range(slots):
        query = q_ref[j]
        own_score = jnp.sum(query * keys_new[j : j + 1], axis=1, keepdims=True) * scale
        scores = dot_t(query.astype(BF16), kc[j]) * scale
        scores = jnp.where(position < lengths[j], scores, -jnp.inf)
        top = jnp.maximum(jnp.max(scores, axis=1, keepdims=True), own_score)
        weights = jnp.exp(scores - top)
        own_weight = jnp.exp(own_score - top)
        totals = jnp.sum(weights, axis=1, keepdims=True) + own_weight
        probs = (weights / totals).astype(BF16)
        own_prob = (own_weight / totals).astype(BF16).astype(F32)
        attended = dot(probs, vc[j]) + own_prob * values_new[j : j + 1]
        for h in range(heads):
            ab[j : j + 1, h * HD : (h + 1) * HD] = attended[h : h + 1]
    ag[w_own] = ab[...].astype(BF16)

    reach = nz // 4

    def z_copy(d, block, to):
        return remote(ag.at[block], ag.at[block], az_s.at[d], az_r.at[d], {"z": to})

    def x_copy(d, e, block, to):
        return remote(ag.at[block], ag.at[block], ax_s.at[d, e], ax_r.at[d, e], {"x": to})

    def block_of(e, d):
        return at_x(nx - e) * nz + at_z(nz - d)

    def along_x(d, hops):
        for e in hops:
            send(x_copy(d, e, block_of(0, d), at_x(e)))

    for k in range(reach, 0, -1):
        send(z_copy(k, w_own, at_z(k)))
        send(z_copy(nz - k, w_own, at_z(nz - k)))
    order = [0] + by_distance(nz)
    near = [d for d in order if min(d, nz - d) <= reach]
    far = [d for d in order if min(d, nz - d) > reach]
    along_x(0, (1, nx - 1))
    for d in (reach, nz - reach):
        z_copy(d, block_of(0, d), z).wait_recv()
        if d == reach:
            for k in range(reach, 0, -1):
                send(z_copy(reach + k, block_of(0, d), at_z(k)))
        else:
            for k in range(reach - 1, 0, -1):
                send(z_copy(nz - reach - k, block_of(0, d), at_z(nz - k)))
    for d in near[1:]:
        if d not in (reach, nz - reach):
            z_copy(d, block_of(0, d), z).wait_recv()
        along_x(d, (1, nx - 1))
    for d in near:
        e = 1 if d % 2 == 0 else nx - 1
        x_copy(d, e, block_of(e, d), x).wait_recv()
        send(x_copy(d, 2, block_of(e, d), at_x(e)))
    for d in far:
        z_copy(d, block_of(0, d), z).wait_recv()
        along_x(d, (1, nx - 1, 2))
    wo_in.wait()
    for d in order:
        passed = 1 if d % 2 == 0 else nx - 1
        for e in range(1, nx):
            if d in far or e != passed:
                x_copy(d, e, block_of(e, d), x).wait_recv()

    group = 16 // slots
    for g in range(rows // 16):
        blocks = [ag[g * group + i].astype(F32) for i in range(group)]
        att[g * 16 : (g + 1) * 16, :] = jnp.concatenate(blocks, axis=0).astype(BF16)
    tile = 512
    update = jnp.zeros((rows, wo.shape[1]), F32)
    for k in range(att.shape[1] // tile):
        picked = dot(pr[...], att[:, k * tile : (k + 1) * tile]).astype(BF16)
        update = update + dot(picked, wo[k * tile : (k + 1) * tile, :])
    total = update.reshape(nn, rows_n, wo.shape[1])
    mine[...] = total
    nst[...] = total.astype(BF16)
    for d in range(1, nn):
        send(remote(nst.at[at_n(d)], nin.at[d], no_s.at[d], no_r.at[d], {"narrow": at_n(d)}))
    result = mine[n]
    for d in range(1, nn):
        src = at_n(nn - d)
        remote(nst.at[0], nin.at[d], no_s.at[d], no_r.at[d], {"narrow": src}).wait_recv()
        result = result + nin[d].astype(F32)
    out_ref[...] = (nres[n, x].astype(F32) + result).astype(BF16)

    for copy in sends:
        copy.wait_send()

    @pl.when(x != 0)
    def _():
        k_copy.wait_send()

    @pl.when(x != nx - 1)
    def _():
        v_copy.wait_send()


def per_device(nx, nz, nn, table, residual, norm_gain, w_query, w_keyval, w_out, cache_rows, lengths, assignment):
    slots, most, _, channels = cache_rows.shape
    kw, query_cols = w_query.shape
    rows_n = residual.shape[0]
    rows = rows_n * nn
    qcols = query_cols // nx
    pieces = qcols // HD + 1
    heads = query_cols // HD
    steps = nz // 4
    width = kw * nx * nz
    anywhere = pl.BlockSpec(memory_space=pl.ANY)
    vmem = pl.BlockSpec(memory_space=pltpu.VMEM)
    smem = pl.BlockSpec(memory_space=pltpu.SMEM)
    dma = pltpu.SemaphoreType.DMA
    scratch = [
        pltpu.VMEM((nn, nx, rows_n, kw), BF16),
        pltpu.VMEM((nx, 1, kw), F32),
        pltpu.VMEM((nx, kw, qcols), BF16),
        pltpu.VMEM((2 * kw, HD), BF16),
        pltpu.VMEM((2, kw, HD), BF16),
        pltpu.VMEM((2, kw, HD), BF16),
        pltpu.VMEM(w_out.shape, BF16),
        pltpu.VMEM((slots * most * 2, HD), BF16),
        pltpu.VMEM((slots, most, HD), BF16),
        pltpu.VMEM((slots, most, HD), BF16),
        pltpu.VMEM(table.shape, F32),
        pltpu.VMEM((kw,), BF16),
        pltpu.VMEM((nz, 1, rows), F32),
        pltpu.VMEM((nn, 1, rows), F32),
        pltpu.VMEM((rows, rows), BF16),
        pltpu.VMEM((rows, rows), BF16),
        pltpu.VMEM((rows, nx * kw), BF16),
        pltpu.VMEM((rows, nx * kw), BF16),
        pltpu.VMEM((nz, pieces, nx * slots, HD), F32),
        pltpu.VMEM((steps, pieces, nx * slots, HD), F32),
        pltpu.VMEM((steps, pieces, nx * slots, HD), F32),
        pltpu.VMEM((steps, pieces, nx * slots, HD), F32),
        pltpu.VMEM((steps, pieces, nx * slots, HD), F32),
        pltpu.VMEM((2, kw // 2, qcols), BF16),
        pltpu.VMEM((nx, pieces, slots, HD), F32),
        pltpu.VMEM((nx, pieces, slots, HD), F32),
        pltpu.VMEM((slots, heads, HD), F32),
        pltpu.VMEM((slots, query_cols), F32),
        pltpu.VMEM((nx * nz, slots, query_cols), BF16),
        pltpu.VMEM((rows, query_cols), BF16),
        pltpu.VMEM((nn, rows_n, w_out.shape[1]), F32),
        pltpu.VMEM((nn, rows_n, w_out.shape[1]), BF16),
        pltpu.VMEM((nn, rows_n, w_out.shape[1]), BF16),
        dma((7,)),
        dma((nx,)), dma((nx,)), dma((nx,)), dma((nx,)), dma((nx,)), dma((nx,)),
        dma((2,)), dma((2,)),
        dma((7,)), dma((7,)),
        dma((nz,)), dma((nz,)),
        dma((nn,)), dma((nn,)),
        *[dma((steps, pieces))] * 8,
        dma((2,)), dma((2,)), dma((2,)), dma((2,)),
        dma((nx, pieces)), dma((nx, pieces)),
        dma((nz,)), dma((nz,)), dma((nz, nx)), dma((nz, nx)),
        dma((nn,)), dma((nn,)),
    ]
    return pl.pallas_call(
        functools.partial(kernel, nx, nz, nn, width),
        out_shape=jax.ShapeDtypeStruct(residual.shape, BF16),
        in_specs=[smem, smem, anywhere, anywhere, vmem] + [anywhere] * 5,
        out_specs=vmem,
        scratch_shapes=scratch,
        compiler_params=pltpu.CompilerParams(
            collective_id=0, has_side_effects=True, vmem_limit_bytes=60 * 1024 * 1024
        ),
        name="decode_block",
    )(
        lengths,
        assignment,
        residual,
        norm_gain,
        assignment.reshape(1, -1),
        w_query,
        w_keyval.reshape(2 * kw, channels),
        w_out,
        cache_rows.reshape(slots * most * 2, channels),
        table,
    )


def solution(mesh):
    nx, nn = 4, mesh.shape["narrow"]
    nz = mesh.shape["wide"] // nx
    torus = Mesh(mesh.devices.reshape(nx, nz, nn), ("x", "z", "narrow"))
    wide = ("x", "z")

    def run(residual, norm_gain, w_query, w_keyval, w_out, cache_rows, lengths, assignment):
        table = jnp.asarray(rotation_table(cache_rows.shape[1]))
        body = jax.shard_map(
            lambda table, *args: per_device(nx, nz, nn, table, *args),
            mesh=torus,
            in_specs=(
                P(),
                P("narrow", wide),
                P(wide),
                P(wide, "narrow"),
                P(wide, None, "narrow"),
                P("narrow", wide),
                P(wide, None, None, "narrow"),
                P(),
                P(),
            ),
            out_specs=P("narrow", wide),
            check_vma=False,
        )
        return body(table, residual, norm_gain, w_query, w_keyval, w_out, cache_rows, lengths, assignment)

    return run
```

```python
import functools
import math

import jax
import jax.numpy as jnp
import numpy as np
from jax import lax
from jax.experimental import pallas as pl
from jax.experimental.pallas import tpu as pltpu
from jax.sharding import Mesh
from jax.sharding import PartitionSpec as P

HD = 128
MESH = pl.DeviceIdType.MESH
F32 = jnp.float32
BF16 = jnp.bfloat16


def rotation_table(most):
    half = HD // 2
    exponents = -(np.arange(half, dtype=np.float32) * np.float32(2.0) / np.float32(HD))
    freqs = np.power(np.float32(500000.0), exponents).astype(np.float32)
    rows = (most + 8) // 8 * 8
    angles = (np.arange(rows, dtype=np.float32)[:, None] * freqs[None, :]).astype(np.float32)
    angles = angles.astype(np.float64)
    return np.concatenate([np.cos(angles), np.sin(angles)], axis=1).astype(np.float32)


def dot(a, b):
    return lax.dot_general(a, b, (((1,), (0,)), ((), ())), preferred_element_type=F32)


def dot_t(a, b):
    return lax.dot_general(a, b, (((1,), (1,)), ((), ())), preferred_element_type=F32)


def by_distance(count):
    return sorted(range(1, count), key=lambda d: min(d, count - d))


def kernel(
    nx, nz, nn, width,
    lens, asg, res_h, gain_h, asg_ref, wq_h, wkv_h, wo_h, cache_h, tab_h,
    out_ref,
    nres, gains, wq, wkv, kvs, kvw, wo, cache, kc, vc, tab,
    gain_v, zin, nsq, pz, pr, sres, nrm, part, r_even, r_odd, l_even, l_odd, wrel, xs, xin, q_ref, ab, ag, att, nst, nin,
    loc, xr_s, xr_r, xg_s, xg_r, xw_s, xw_r, kv_s, kv_r, ng_s, ng_r,
    zs_s, zs_r, ns_s, ns_r, re_s, re_r, ro_s, ro_r, le_s, le_r, lo_s, lo_r, wr_s, wr_r, wf_s, wf_r, xe_s, xe_r,
    az_s, az_r, ax_s, ax_r, no_s, no_r,
):
    x, z, n = lax.axis_index("x"), lax.axis_index("z"), lax.axis_index("narrow")
    y, c = n // 2, n % 2
    ny = nn // 2
    turn = 1 - 2 * c
    rows = pz.shape[0]
    rows_n = rows // nn
    slots = xs.shape[2]
    per_z = nx * slots
    pieces = part.shape[1]
    qcols = wq.shape[2]
    kw = wq.shape[1]
    most = kc.shape[1]
    heads = q_ref.shape[1]
    heads_x = heads // nx
    w_own = x * nz + z

    def remote(src, dst, ss, rs, dev):
        return pltpu.make_async_remote_copy(
            src_ref=src, dst_ref=dst, send_sem=ss, recv_sem=rs, device_id=dev, device_id_type=MESH
        )

    def at_x(d):
        return lax.rem(x + d, nx)

    def at_z(d):
        return lax.rem(z + d, nz)

    def at_n(d):
        return lax.rem(n + d, nn)

    def wq_part(t):
        return wq_h.at[:, pl.ds(pl.multiple_of(t * qcols, qcols), qcols)]

    far_first = sorted(range(1, nn), key=lambda d: -min(d // 2, (nn - d) // 2))
    local = [
        pltpu.make_async_copy(gain_h, gain_v, loc.at[6]),
        pltpu.make_async_copy(wkv_h, wkv, loc.at[0]),
        pltpu.make_async_copy(res_h, nres.at[n, x], loc.at[1]),
        pltpu.make_async_copy(wq_part(x), wq.at[x], loc.at[2]),
        pltpu.make_async_copy(cache_h, cache, loc.at[3]),
        pltpu.make_async_copy(wo_h, wo, loc.at[4]),
        pltpu.make_async_copy(tab_h, tab, loc.at[5]),
    ]
    barrier = pltpu.get_barrier_semaphore()
    reach = nz // 4
    z_near = [d for d in by_distance(nz) if min(d, nz - d) <= reach]
    for d in reversed(z_near):
        pl.semaphore_signal(barrier, inc=1, device_id={"z": at_z(d)}, device_id_type=MESH)
    for d in range(1, nx):
        pl.semaphore_signal(barrier, inc=1, device_id={"x": at_x(d)}, device_id_type=MESH)
    for d in range(1, nn):
        pl.semaphore_signal(barrier, inc=1, device_id={"narrow": at_n(d)}, device_id_type=MESH)
    for copy in local:
        copy.start()
    gain_in, wkv_in, res_in, wq_in, cache_in, wo_in, tab_in = local
    pl.semaphore_wait(barrier, (nx - 1) + len(z_near) + (nn - 1))

    sends = []

    def send(copy):
        copy.start()
        sends.append(copy)

    def relay_half(i, src, to):
        return remote(src, wrel.at[i], wr_s.at[i], wr_r.at[i], {"x": to})

    def relayed(i, owner, to):
        half = wq.at[owner, i * (kw // 2) : (i + 1) * (kw // 2)]
        return remote(wrel.at[i], half, wf_s.at[i], wf_r.at[i], {"x": to})

    for d in (2, 1, nx - 1):
        send(remote(res_h, nres.at[n, x], xr_s.at[d], xr_r.at[d], {"x": at_x(d)}))
    gain_in.wait()
    gains[x] = gain_v[...].astype(F32).reshape(1, kw)
    for d in range(1, nx):
        send(remote(gains.at[x], gains.at[x], xg_s.at[d], xg_r.at[d], {"x": at_x(d)}))
    far_cols = pl.ds(pl.multiple_of(at_x(2) * qcols, qcols), qcols)
    send(relay_half(0, wq_h.at[0 : kw // 2, far_cols], at_x(1)))
    send(relay_half(1, wq_h.at[kw // 2 : kw, far_cols], at_x(nx - 1)))
    for d in (1, nx - 1):
        send(remote(wq_part(at_x(d)), wq.at[x], xw_s.at[d], xw_r.at[d], {"x": at_x(d)}))

    a_row = asg_ref[...]
    i_sub = lax.broadcasted_iota(jnp.int32, (rows, rows), 0)
    i_lane = lax.broadcasted_iota(jnp.int32, (rows, rows), 1)
    zz, rest = i_sub // per_z, i_sub % per_z
    slot_of = ((rest // slots) * nz + zz) * slots + rest % slots
    a_col = jnp.sum(
        jnp.where(i_lane == slot_of, a_row.astype(F32), 0.0), axis=1, keepdims=True
    ).astype(jnp.int32)
    pick = i_lane == a_col
    pz[...] = jnp.where(pick, 1.0, 0.0).astype(BF16)
    pr[...] = jnp.where(i_sub == a_row, 1.0, 0.0).astype(BF16)

    e_row = lax.broadcasted_iota(jnp.int32, (kw, 2 * kw), 0)
    e_col = lax.broadcasted_iota(jnp.int32, (kw, 2 * kw), 1)
    e0 = jnp.where(e_col == 2 * e_row, 1.0, 0.0).astype(BF16)
    e1 = jnp.where(e_col == 2 * e_row + 1, 1.0, 0.0).astype(BF16)
    wkv_in.wait()
    kvs[0] = dot(e0, wkv[...]).astype(BF16)
    kvs[1] = dot(e1, wkv[...]).astype(BF16)

    kv_slot = lax.rem(x, 2)
    k_copy = remote(kvs.at[0], kvw.at[kv_slot], kv_s.at[0], kv_r.at[kv_slot], {"x": x // 2})
    v_copy = remote(kvs.at[1], kvw.at[kv_slot], kv_s.at[1], kv_r.at[kv_slot], {"x": 2 + x // 2})

    @pl.when(x != 0)
    def _():
        k_copy.start()

    @pl.when(x == 0)
    def _():
        kvw[0] = kvs[0]

    @pl.when(x != nx - 1)
    def _():
        v_copy.start()

    @pl.when(x == nx - 1)
    def _():
        kvw[1] = kvs[1]

    def narrow(dy, core):
        return lax.rem(y + dy + ny, ny) * 2 + core

    def row_copy(k, src, to):
        return remote(nres.at[src], nres.at[src], ng_s.at[k], ng_r.at[k], {"narrow": to})

    res_in.wait()
    for d in range(1, nx):
        src = at_x(nx - d)
        remote(res_h, nres.at[n, src], xr_s.at[d], xr_r.at[d], {"x": src}).wait_recv()
    ahead, behind, across = narrow(turn, c), narrow(-turn, c), narrow(2, c)
    other = narrow(0, 1 - c)
    send(row_copy(0, n, ahead))
    send(row_copy(1, n, behind))
    send(row_copy(3, n, other))

    squares = jnp.zeros((rows_n, 1), F32)
    for k in range(nx):
        block = nres[n, k].astype(F32)
        squares = squares + jnp.sum(block * block, axis=1, keepdims=True)
    r_sub = lax.broadcasted_iota(jnp.int32, (rows_n, rows), 0)
    r_lane = lax.broadcasted_iota(jnp.int32, (rows_n, rows), 1)
    zin[z] = jnp.sum(jnp.where(r_lane == r_sub + n * rows_n, squares, 0.0), axis=0, keepdims=True)

    def sum_copy(d, src, to):
        return remote(zin.at[src], zin.at[src], zs_s.at[d], zs_r.at[d], {"z": to})

    for d in reversed(z_near):
        send(sum_copy(d, z, at_z(d)))

    cache_in.wait()
    step = kw
    for j in range(slots):
        for b in range(most // step):
            block = cache[pl.ds((j * most + b * step) * 2, 2 * step), :]
            kc[j, b * step : (b + 1) * step, :] = dot(e0, block).astype(BF16)
            vc[j, b * step : (b + 1) * step, :] = dot(e1, block).astype(BF16)

    src = at_z(nz - reach)
    sum_copy(reach, src, z).wait_recv()
    for k in range(reach, 0, -1):
        send(sum_copy(reach + k, src, at_z(k)))
    src = at_z(reach)
    sum_copy(nz - reach, src, z).wait_recv()
    for k in range(reach - 1, 0, -1):
        send(sum_copy(nz - reach - k, src, at_z(nz - k)))

    left_x, right_x, opposite = at_x(nx - 1), at_x(1), at_x(2)
    relay_half(0, wrel.at[0], left_x).wait_recv()
    send(relayed(0, left_x, right_x))
    relay_half(1, wrel.at[1], right_x).wait_recv()
    send(relayed(1, right_x, left_x))

    row_copy(0, behind, behind).wait_recv()
    send(row_copy(2, behind, ahead))
    send(row_copy(4, behind, other))
    row_copy(1, ahead, ahead).wait_recv()
    send(row_copy(5, ahead, other))
    row_copy(2, across, behind).wait_recv()
    send(row_copy(6, across, other))

    for d in range(1, nz):
        if d in (reach, nz - reach):
            continue
        src = at_z(nz - d)
        remote(zin.at[src], zin.at[src], zs_s.at[d], zs_r.at[d], {"z": src}).wait_recv()
    nsq[n] = jnp.sum(zin[...], axis=0)
    for d in far_first:
        send(remote(nsq.at[n], nsq.at[n], ns_s.at[d], ns_r.at[d], {"narrow": at_n(d)}))

    far = narrow(-2 * turn, 1 - c)
    for k, src in ((3, other), (4, narrow(turn, 1 - c)), (5, narrow(-turn, 1 - c)), (6, far)):
        row_copy(k, src, other).wait_recv()
    for k in range(nx):
        block = nres[:, k].reshape(rows, kw)
        sres[:, k * kw : (k + 1) * kw] = dot(pz[...], block).astype(BF16)

    for d in range(1, nn):
        src = at_n(nn - d)
        remote(nsq.at[src], nsq.at[src], ns_s.at[d], ns_r.at[d], {"narrow": src}).wait_recv()
    sums = jnp.sum(nsq[...], axis=0)
    sum_col = jnp.sum(jnp.where(pz[...].astype(F32) > 0.5, sums, 0.0), axis=1, keepdims=True)
    inverse = lax.rsqrt(sum_col / width + 1e-05)

    for d in range(1, nx):
        src = at_x(nx - d)
        remote(gains.at[src], gains.at[src], xg_s.at[d], xg_r.at[d], {"x": src}).wait_recv()
    for k in range(nx):
        block = sres[:, k * kw : (k + 1) * kw].astype(F32)
        nrm[:, k * kw : (k + 1) * kw] = (block * inverse * gains[k]).astype(BF16)

    wq_in.wait()
    for d in (1, nx - 1):
        src = at_x(nx - d)
        remote(wq_part(src), wq.at[src], xw_s.at[d], xw_r.at[d], {"x": src}).wait_recv()
    relayed(0, opposite, left_x).wait_recv()
    relayed(1, opposite, right_x).wait_recv()

    @pl.when(x != 0)
    def _():
        remote(kvs.at[0], kvw.at[0], kv_s.at[0], kv_r.at[0], {"x": x // 2}).wait_recv()

    @pl.when(x != nx - 1)
    def _():
        remote(kvs.at[0], kvw.at[1], kv_s.at[0], kv_r.at[1], {"x": x // 2}).wait_recv()

    steps = nz // 4
    sides = ((1, r_even, r_odd, re_s, re_r, ro_s, ro_r), (-1, l_even, l_odd, le_s, le_r, lo_s, lo_r))

    def along(side, d):
        return at_z(d if side[0] > 0 else nz - d)

    def odd_copy(side, i, k):
        src = part.at[along(side, 2 * i + 1), k]
        to = {"z": along(side, 1)}
        return remote(src, side[2].at[i, k], side[5].at[i, k], side[6].at[i, k], to)

    def even_copy(side, s, k):
        if s == 0:
            src = part.at[along(side, 2 * steps), k]
        elif s == 1 and side[0] < 0:
            src = side[2].at[steps - 1, k]
        else:
            src = side[1].at[s - 1, k]
        to = {"z": along(side, 2)}
        return remote(src, side[1].at[s, k], side[3].at[s, k], side[4].at[s, k], to)

    def start_piece(k):
        send(even_copy(sides[0], 0, k))
        for side in sides:
            send(odd_copy(side, steps - 1, k))

    for k in range(0, pieces - 1, 2):
        cols = slice(k * HD, (k + 2) * HD)
        total = dot(nrm[:, :kw], wq[0, :, cols])
        for t in range(1, nx):
            total = total + dot(nrm[:, t * kw : (t + 1) * kw], wq[t, :, cols])
        for h in range(2):
            part[:, k + h] = total[:, h * HD : (h + 1) * HD].reshape(nz, per_z, HD)
            start_piece(k + h)
    half = nrm[:, pl.ds(pl.multiple_of(lax.rem(x, 2) * 2 * kw, 2 * kw), 2 * kw)]
    kv_part = dot(half[:, :kw], kvw[0]) + dot(half[:, kw:], kvw[1])
    part[:, pieces - 1] = kv_part.reshape(nz, per_z, HD)
    start_piece(pieces - 1)
    for k in range(pieces):
        for side in sides:
            send(odd_copy(side, steps - 2, k))
    for s in range(1, steps):
        for k in range(pieces):
            for side in sides:
                own_part = part[along(side, 2 * (steps - s)), k]
                odd_copy(side, steps - s, k).wait_recv()
                if s == 1 and side[0] < 0:
                    side[2][steps - 1, k] = side[2][steps - 1, k] + own_part
                else:
                    even_copy(side, s - 1, k).wait_recv()
                    side[1][s - 1, k] = side[1][s - 1, k] + side[2][steps - s, k] + own_part
                send(even_copy(side, s, k))
        if s + 1 < steps:
            for k in range(pieces):
                for side in sides:
                    send(odd_copy(side, steps - s - 2, k))
    for k in range(pieces):
        own = part[z, k]
        for side in sides:
            odd_copy(side, 0, k).wait_recv()
            even_copy(side, steps - 1, k).wait_recv()
            own = own + side[1][steps - 1, k] + side[2][0, k]
        for t in range(nx):
            xs[t, k] = own[t * slots : (t + 1) * slots]
        for d in (2, 1, nx - 1):
            to = at_x(d)
            send(remote(xs.at[to, k], xin.at[x, k], xe_s.at[d, k], xe_r.at[d, k], {"x": to}))
    xin[x] = xs[x]

    tab_in.wait()
    lengths = [lens[asg[w_own * slots + j]] for j in range(slots)]
    angles = jnp.concatenate([tab[pl.ds(lengths[j], 1), :] for j in range(slots)], axis=0)
    turned = pltpu.roll(angles, HD // 2, 1)
    lane = lax.broadcasted_iota(jnp.int32, (slots, HD), 1)
    cosine = jnp.where(lane < HD // 2, angles, turned)
    sine = jnp.where(lane < HD // 2, -turned, angles)

    def rotate(v):
        return (v * cosine + pltpu.roll(v, HD // 2, 1) * sine).astype(BF16).astype(F32)

    for i in range(pieces):
        for d in range(1, nx):
            src = at_x(nx - d)
            remote(xs.at[0, i], xin.at[src, i], xe_s.at[d, i], xe_r.at[d, i], {"x": src}).wait_recv()
        for k in range(nx if i < heads_x else 0):
            turned_query = rotate(xin[k, i])
            for j in range(slots):
                q_ref[j, k * heads_x + i : k * heads_x + i + 1, :] = turned_query[j : j + 1]
    keys_new = rotate(xin[0, pieces - 1] + xin[1, pieces - 1])
    values_new = (xin[2, pieces - 1] + xin[3, pieces - 1]).astype(BF16).astype(F32)

    scale = 1.0 / math.sqrt(HD)
    position = lax.broadcasted_iota(jnp.int32, (heads, most), 1)
    for j in range(slots):
        query = q_ref[j]
        own_score = jnp.sum(query * keys_new[j : j + 1], axis=1, keepdims=True) * scale
        scores = dot_t(query.astype(BF16), kc[j]) * scale
        scores = jnp.where(position < lengths[j], scores, -jnp.inf)
        top = jnp.maximum(jnp.max(scores, axis=1, keepdims=True), own_score)
        weights = jnp.exp(scores - top)
        own_weight = jnp.exp(own_score - top)
        totals = jnp.sum(weights, axis=1, keepdims=True) + own_weight
        probs = (weights / totals).astype(BF16)
        own_prob = (own_weight / totals).astype(BF16).astype(F32)
        attended = dot(probs, vc[j]) + own_prob * values_new[j : j + 1]
        for h in range(heads):
            ab[j : j + 1, h * HD : (h + 1) * HD] = attended[h : h + 1]
    ag[w_own] = ab[...].astype(BF16)

    def z_copy(d, block, to):
        return remote(ag.at[block], ag.at[block], az_s.at[d], az_r.at[d], {"z": to})

    def x_copy(d, e, block, to):
        return remote(ag.at[block], ag.at[block], ax_s.at[d, e], ax_r.at[d, e], {"x": to})

    def block_of(e, d):
        return at_x(nx - e) * nz + at_z(nz - d)

    def along_x(d, hops):
        for e in hops:
            send(x_copy(d, e, block_of(0, d), at_x(e)))

    for k in range(reach, 0, -1):
        send(z_copy(k, w_own, at_z(k)))
        send(z_copy(nz - k, w_own, at_z(nz - k)))
    order = [0] + by_distance(nz)
    near = [d for d in order if min(d, nz - d) <= reach]
    far = [d for d in order if min(d, nz - d) > reach]
    along_x(0, (1, nx - 1))
    for d in (reach, nz - reach):
        z_copy(d, block_of(0, d), z).wait_recv()
        if d == reach:
            for k in range(reach, 0, -1):
                send(z_copy(reach + k, block_of(0, d), at_z(k)))
        else:
            for k in range(reach - 1, 0, -1):
                send(z_copy(nz - reach - k, block_of(0, d), at_z(nz - k)))
    for d in near[1:]:
        if d not in (reach, nz - reach):
            z_copy(d, block_of(0, d), z).wait_recv()
        along_x(d, (1, nx - 1))
    for d in near:
        e = 1 if d % 2 == 0 else nx - 1
        x_copy(d, e, block_of(e, d), x).wait_recv()
        send(x_copy(d, 2, block_of(e, d), at_x(e)))
    for d in far:
        z_copy(d, block_of(0, d), z).wait_recv()
        along_x(d, (1, nx - 1, 2))
    wo_in.wait()
    for d in order:
        passed = 1 if d % 2 == 0 else nx - 1
        for e in range(1, nx):
            if d in far or e != passed:
                x_copy(d, e, block_of(e, d), x).wait_recv()

    group = 16 // slots
    for g in range(rows // 16):
        blocks = [ag[g * group + i].astype(F32) for i in range(group)]
        att[g * 16 : (g + 1) * 16, :] = jnp.concatenate(blocks, axis=0).astype(BF16)
    tile = 512
    update = jnp.zeros((rows, wo.shape[1]), F32)
    for k in range(att.shape[1] // tile):
        cols = slice(k * tile, (k + 1) * tile)
        update = update + dot(att[:, cols], wo[cols, :])
    rounded = update.astype(BF16)
    rest = (update - rounded.astype(F32)).astype(BF16)
    picked = dot(pr[...], rounded)
    nst[...] = picked.astype(BF16).reshape(nn, rows_n, wo.shape[1])
    for d in far_first:
        send(remote(nst.at[at_n(d)], nin.at[d], no_s.at[d], no_r.at[d], {"narrow": at_n(d)}))
    own_pick = pr[pl.ds(pl.multiple_of(n * rows_n, rows_n), rows_n), :]
    result = nst[n].astype(F32) + dot(own_pick, rest)
    for d in range(1, nn):
        src = at_n(nn - d)
        remote(nst.at[0], nin.at[d], no_s.at[d], no_r.at[d], {"narrow": src}).wait_recv()
        result = result + nin[d].astype(F32)
    out_ref[...] = (nres[n, x].astype(F32) + result).astype(BF16)

    for copy in sends:
        copy.wait_send()

    @pl.when(x != 0)
    def _():
        k_copy.wait_send()

    @pl.when(x != nx - 1)
    def _():
        v_copy.wait_send()


def per_device(nx, nz, nn, table, residual, norm_gain, w_query, w_keyval, w_out, cache_rows, lengths, assignment):
    slots, most, _, channels = cache_rows.shape
    kw, query_cols = w_query.shape
    rows_n = residual.shape[0]
    rows = rows_n * nn
    qcols = query_cols // nx
    pieces = qcols // HD + 1
    heads = query_cols // HD
    steps = nz // 4
    width = kw * nx * nz
    anywhere = pl.BlockSpec(memory_space=pl.ANY)
    vmem = pl.BlockSpec(memory_space=pltpu.VMEM)
    smem = pl.BlockSpec(memory_space=pltpu.SMEM)
    dma = pltpu.SemaphoreType.DMA
    scratch = [
        pltpu.VMEM((nn, nx, rows_n, kw), BF16),
        pltpu.VMEM((nx, 1, kw), F32),
        pltpu.VMEM((nx, kw, qcols), BF16),
        pltpu.VMEM((2 * kw, HD), BF16),
        pltpu.VMEM((2, kw, HD), BF16),
        pltpu.VMEM((2, kw, HD), BF16),
        pltpu.VMEM(w_out.shape, BF16),
        pltpu.VMEM((slots * most * 2, HD), BF16),
        pltpu.VMEM((slots, most, HD), BF16),
        pltpu.VMEM((slots, most, HD), BF16),
        pltpu.VMEM(table.shape, F32),
        pltpu.VMEM((kw,), BF16),
        pltpu.VMEM((nz, 1, rows), F32),
        pltpu.VMEM((nn, 1, rows), F32),
        pltpu.VMEM((rows, rows), BF16),
        pltpu.VMEM((rows, rows), BF16),
        pltpu.VMEM((rows, nx * kw), BF16),
        pltpu.VMEM((rows, nx * kw), BF16),
        pltpu.VMEM((nz, pieces, nx * slots, HD), F32),
        pltpu.VMEM((steps, pieces, nx * slots, HD), F32),
        pltpu.VMEM((steps, pieces, nx * slots, HD), F32),
        pltpu.VMEM((steps, pieces, nx * slots, HD), F32),
        pltpu.VMEM((steps, pieces, nx * slots, HD), F32),
        pltpu.VMEM((2, kw // 2, qcols), BF16),
        pltpu.VMEM((nx, pieces, slots, HD), F32),
        pltpu.VMEM((nx, pieces, slots, HD), F32),
        pltpu.VMEM((slots, heads, HD), F32),
        pltpu.VMEM((slots, query_cols), F32),
        pltpu.VMEM((nx * nz, slots, query_cols), BF16),
        pltpu.VMEM((rows, query_cols), BF16),
        pltpu.VMEM((nn, rows_n, w_out.shape[1]), BF16),
        pltpu.VMEM((nn, rows_n, w_out.shape[1]), BF16),
        dma((7,)),
        dma((nx,)), dma((nx,)), dma((nx,)), dma((nx,)), dma((nx,)), dma((nx,)),
        dma((2,)), dma((2,)),
        dma((7,)), dma((7,)),
        dma((nz,)), dma((nz,)),
        dma((nn,)), dma((nn,)),
        *[dma((steps, pieces))] * 8,
        dma((2,)), dma((2,)), dma((2,)), dma((2,)),
        dma((nx, pieces)), dma((nx, pieces)),
        dma((nz,)), dma((nz,)), dma((nz, nx)), dma((nz, nx)),
        dma((nn,)), dma((nn,)),
    ]
    return pl.pallas_call(
        functools.partial(kernel, nx, nz, nn, width),
        out_shape=jax.ShapeDtypeStruct(residual.shape, BF16),
        in_specs=[smem, smem, anywhere, anywhere, vmem] + [anywhere] * 5,
        out_specs=vmem,
        scratch_shapes=scratch,
        compiler_params=pltpu.CompilerParams(
            collective_id=0, has_side_effects=True, vmem_limit_bytes=60 * 1024 * 1024
        ),
        name="decode_block",
    )(
        lengths,
        assignment,
        residual,
        norm_gain,
        assignment.reshape(1, -1),
        w_query,
        w_keyval.reshape(2 * kw, channels),
        w_out,
        cache_rows.reshape(slots * most * 2, channels),
        table,
    )


def solution(mesh):
    nx, nn = 4, mesh.shape["narrow"]
    nz = mesh.shape["wide"] // nx
    torus = Mesh(mesh.devices.reshape(nx, nz, nn), ("x", "z", "narrow"))
    wide = ("x", "z")

    def run(residual, norm_gain, w_query, w_keyval, w_out, cache_rows, lengths, assignment):
        table = jnp.asarray(rotation_table(cache_rows.shape[1]))
        body = jax.shard_map(
            lambda table, *args: per_device(nx, nz, nn, table, *args),
            mesh=torus,
            in_specs=(
                P(),
                P("narrow", wide),
                P(wide),
                P(wide, "narrow"),
                P(wide, None, "narrow"),
                P("narrow", wide),
                P(wide, None, None, "narrow"),
                P(),
                P(),
            ),
            out_specs=P("narrow", wide),
            check_vma=False,
        )
        return body(table, residual, norm_gain, w_query, w_keyval, w_out, cache_rows, lengths, assignment)

    return run
```

```python
import functools
import math

import jax
import jax.numpy as jnp
import numpy as np
from jax import lax
from jax.experimental import pallas as pl
from jax.experimental.pallas import tpu as pltpu
from jax.sharding import Mesh
from jax.sharding import PartitionSpec as P

HD = 128
MESH = pl.DeviceIdType.MESH
F32 = jnp.float32
BF16 = jnp.bfloat16


def rotation_table(most):
    half = HD // 2
    exponents = -(np.arange(half, dtype=np.float32) * np.float32(2.0) / np.float32(HD))
    freqs = np.power(np.float32(500000.0), exponents).astype(np.float32)
    rows = (most + 8) // 8 * 8
    angles = (np.arange(rows, dtype=np.float32)[:, None] * freqs[None, :]).astype(np.float32)
    angles = angles.astype(np.float64)
    return np.concatenate([np.cos(angles), np.sin(angles)], axis=1).astype(np.float32)


def dot(a, b):
    return lax.dot_general(a, b, (((1,), (0,)), ((), ())), preferred_element_type=F32)


def dot_t(a, b):
    return lax.dot_general(a, b, (((1,), (1,)), ((), ())), preferred_element_type=F32)


def by_distance(count):
    return sorted(range(1, count), key=lambda d: min(d, count - d))


def kernel(
    nx, nz, nn, width,
    lens, asg, res_h, gain_h, asg_ref, wq_h, wkv_h, wo_h, cache_h, tab_h,
    out_ref,
    nres, gains, wq, wkv, kvs, kvw, wo, cache, kc, vc, tab,
    gain_v, zin, nsq, pz, pr, sres, nrm, part, r_even, r_odd, l_even, l_odd, wrel, xs, xin, q_ref, ab, ag, att, nst, nin,
    loc, xr_s, xr_r, xg_s, xg_r, xw_s, xw_r, kv_s, kv_r, ng_s, ng_r,
    zs_s, zs_r, ns_s, ns_r, re_s, re_r, ro_s, ro_r, le_s, le_r, lo_s, lo_r, wr_s, wr_r, wf_s, wf_r, xe_s, xe_r,
    az_s, az_r, ax_s, ax_r, no_s, no_r,
):
    x, z, n = lax.axis_index("x"), lax.axis_index("z"), lax.axis_index("narrow")
    y, c = n // 2, n % 2
    ny = nn // 2
    turn = 1 - 2 * c
    rows = pz.shape[0]
    rows_n = rows // nn
    slots = xs.shape[2]
    per_z = nx * slots
    pieces = part.shape[1]
    qcols = wq.shape[2]
    kw = wq.shape[1]
    most = kc.shape[1]
    heads = q_ref.shape[1]
    heads_x = heads // nx
    w_own = x * nz + z

    def remote(src, dst, ss, rs, dev):
        return pltpu.make_async_remote_copy(
            src_ref=src, dst_ref=dst, send_sem=ss, recv_sem=rs, device_id=dev, device_id_type=MESH
        )

    def at_x(d):
        return lax.rem(x + d, nx)

    def at_z(d):
        return lax.rem(z + d, nz)

    def at_n(d):
        return lax.rem(n + d, nn)

    def wq_part(t):
        return wq_h.at[:, pl.ds(pl.multiple_of(t * qcols, qcols), qcols)]

    far_first = sorted(range(1, nn), key=lambda d: -min(d // 2, (nn - d) // 2))
    local = [
        pltpu.make_async_copy(gain_h, gain_v, loc.at[6]),
        pltpu.make_async_copy(wkv_h, wkv, loc.at[0]),
        pltpu.make_async_copy(res_h, nres.at[n, x], loc.at[1]),
        pltpu.make_async_copy(wq_part(x), wq.at[x], loc.at[2]),
        pltpu.make_async_copy(cache_h, cache, loc.at[3]),
        pltpu.make_async_copy(wo_h, wo, loc.at[4]),
        pltpu.make_async_copy(tab_h, tab, loc.at[5]),
    ]
    barrier = pltpu.get_barrier_semaphore()
    reach = nz // 4
    z_near = [d for d in by_distance(nz) if min(d, nz - d) <= reach]
    for d in reversed(z_near):
        pl.semaphore_signal(barrier, inc=1, device_id={"z": at_z(d)}, device_id_type=MESH)
    for d in range(1, nx):
        pl.semaphore_signal(barrier, inc=1, device_id={"x": at_x(d)}, device_id_type=MESH)
    for d in range(1, nn):
        pl.semaphore_signal(barrier, inc=1, device_id={"narrow": at_n(d)}, device_id_type=MESH)
    for copy in local:
        copy.start()
    gain_in, wkv_in, res_in, wq_in, cache_in, wo_in, tab_in = local
    pl.semaphore_wait(barrier, (nx - 1) + len(z_near) + (nn - 1))

    sends = []

    def send(copy):
        copy.start()
        sends.append(copy)

    def relay_half(i, src, to):
        return remote(src, wrel.at[i], wr_s.at[i], wr_r.at[i], {"x": to})

    def relayed(i, owner, to):
        half = wq.at[owner, i * (kw // 2) : (i + 1) * (kw // 2)]
        return remote(wrel.at[i], half, wf_s.at[i], wf_r.at[i], {"x": to})

    for d in (2, 1, nx - 1):
        send(remote(res_h, nres.at[n, x], xr_s.at[d], xr_r.at[d], {"x": at_x(d)}))
    gain_in.wait()
    gains[x] = gain_v[...].astype(F32).reshape(1, kw)
    for d in range(1, nx):
        send(remote(gains.at[x], gains.at[x], xg_s.at[d], xg_r.at[d], {"x": at_x(d)}))
    far_cols = pl.ds(pl.multiple_of(at_x(2) * qcols, qcols), qcols)
    send(relay_half(0, wq_h.at[0 : kw // 2, far_cols], at_x(1)))
    send(relay_half(1, wq_h.at[kw // 2 : kw, far_cols], at_x(nx - 1)))
    for d in (1, nx - 1):
        send(remote(wq_part(at_x(d)), wq.at[x], xw_s.at[d], xw_r.at[d], {"x": at_x(d)}))

    a_row = asg_ref[...]
    i_sub = lax.broadcasted_iota(jnp.int32, (rows, rows), 0)
    i_lane = lax.broadcasted_iota(jnp.int32, (rows, rows), 1)
    zz, rest = i_sub // per_z, i_sub % per_z
    slot_of = ((rest // slots) * nz + zz) * slots + rest % slots
    a_col = jnp.sum(
        jnp.where(i_lane == slot_of, a_row.astype(F32), 0.0), axis=1, keepdims=True
    ).astype(jnp.int32)
    pick = i_lane == a_col
    pz[...] = jnp.where(pick, 1.0, 0.0).astype(BF16)
    pr[...] = jnp.where(i_sub == a_row, 1.0, 0.0).astype(BF16)

    e_row = lax.broadcasted_iota(jnp.int32, (kw, 2 * kw), 0)
    e_col = lax.broadcasted_iota(jnp.int32, (kw, 2 * kw), 1)
    e0 = jnp.where(e_col == 2 * e_row, 1.0, 0.0).astype(BF16)
    e1 = jnp.where(e_col == 2 * e_row + 1, 1.0, 0.0).astype(BF16)
    wkv_in.wait()
    kvs[0] = dot(e0, wkv[...]).astype(BF16)
    kvs[1] = dot(e1, wkv[...]).astype(BF16)

    kv_slot = lax.rem(x, 2)
    k_copy = remote(kvs.at[0], kvw.at[kv_slot], kv_s.at[0], kv_r.at[kv_slot], {"x": x // 2})
    v_copy = remote(kvs.at[1], kvw.at[kv_slot], kv_s.at[1], kv_r.at[kv_slot], {"x": 2 + x // 2})

    @pl.when(x != 0)
    def _():
        k_copy.start()

    @pl.when(x == 0)
    def _():
        kvw[0] = kvs[0]

    @pl.when(x != nx - 1)
    def _():
        v_copy.start()

    @pl.when(x == nx - 1)
    def _():
        kvw[1] = kvs[1]

    def narrow(dy, core):
        return lax.rem(y + dy + ny, ny) * 2 + core

    def row_copy(k, src, to):
        return remote(nres.at[src], nres.at[src], ng_s.at[k], ng_r.at[k], {"narrow": to})

    res_in.wait()
    for d in range(1, nx):
        src = at_x(nx - d)
        remote(res_h, nres.at[n, src], xr_s.at[d], xr_r.at[d], {"x": src}).wait_recv()
    ahead, behind, across = narrow(turn, c), narrow(-turn, c), narrow(2, c)
    other = narrow(0, 1 - c)
    send(row_copy(0, n, ahead))
    send(row_copy(1, n, behind))
    send(row_copy(3, n, other))

    squares = jnp.zeros((rows_n, 1), F32)
    for k in range(nx):
        block = nres[n, k].astype(F32)
        squares = squares + jnp.sum(block * block, axis=1, keepdims=True)
    r_sub = lax.broadcasted_iota(jnp.int32, (rows_n, rows), 0)
    r_lane = lax.broadcasted_iota(jnp.int32, (rows_n, rows), 1)
    zin[z] = jnp.sum(jnp.where(r_lane == r_sub + n * rows_n, squares, 0.0), axis=0, keepdims=True)

    def sum_copy(d, src, to):
        return remote(zin.at[src], zin.at[src], zs_s.at[d], zs_r.at[d], {"z": to})

    for d in reversed(z_near):
        send(sum_copy(d, z, at_z(d)))

    cache_in.wait()
    step = kw
    for j in range(slots):
        for b in range(most // step):
            block = cache[pl.ds((j * most + b * step) * 2, 2 * step), :]
            kc[j, b * step : (b + 1) * step, :] = dot(e0, block).astype(BF16)
            vc[j, b * step : (b + 1) * step, :] = dot(e1, block).astype(BF16)

    src = at_z(nz - reach)
    sum_copy(reach, src, z).wait_recv()
    for k in range(reach, 0, -1):
        send(sum_copy(reach + k, src, at_z(k)))
    src = at_z(reach)
    sum_copy(nz - reach, src, z).wait_recv()
    for k in range(reach - 1, 0, -1):
        send(sum_copy(nz - reach - k, src, at_z(nz - k)))

    left_x, right_x, opposite = at_x(nx - 1), at_x(1), at_x(2)
    relay_half(0, wrel.at[0], left_x).wait_recv()
    send(relayed(0, left_x, right_x))
    relay_half(1, wrel.at[1], right_x).wait_recv()
    send(relayed(1, right_x, left_x))

    row_copy(0, behind, behind).wait_recv()
    send(row_copy(2, behind, ahead))
    send(row_copy(4, behind, other))
    row_copy(1, ahead, ahead).wait_recv()
    send(row_copy(5, ahead, other))
    row_copy(2, across, behind).wait_recv()
    send(row_copy(6, across, other))

    for d in range(1, nz):
        if d in (reach, nz - reach):
            continue
        src = at_z(nz - d)
        remote(zin.at[src], zin.at[src], zs_s.at[d], zs_r.at[d], {"z": src}).wait_recv()
    nsq[n] = jnp.sum(zin[...], axis=0)
    for d in far_first:
        send(remote(nsq.at[n], nsq.at[n], ns_s.at[d], ns_r.at[d], {"narrow": at_n(d)}))

    far = narrow(-2 * turn, 1 - c)
    for k, src in ((3, other), (4, narrow(turn, 1 - c)), (5, narrow(-turn, 1 - c)), (6, far)):
        row_copy(k, src, other).wait_recv()
    for k in range(nx):
        block = nres[:, k].reshape(rows, kw)
        sres[:, k * kw : (k + 1) * kw] = dot(pz[...], block).astype(BF16)

    for d in range(1, nn):
        src = at_n(nn - d)
        remote(nsq.at[src], nsq.at[src], ns_s.at[d], ns_r.at[d], {"narrow": src}).wait_recv()
    sums = jnp.sum(nsq[...], axis=0)
    sum_col = jnp.sum(jnp.where(pz[...].astype(F32) > 0.5, sums, 0.0), axis=1, keepdims=True)
    inverse = lax.rsqrt(sum_col / width + 1e-05)

    for d in range(1, nx):
        src = at_x(nx - d)
        remote(gains.at[src], gains.at[src], xg_s.at[d], xg_r.at[d], {"x": src}).wait_recv()
    for k in range(nx):
        block = sres[:, k * kw : (k + 1) * kw].astype(F32)
        nrm[:, k * kw : (k + 1) * kw] = (block * inverse * gains[k]).astype(BF16)

    wq_in.wait()
    for d in (1, nx - 1):
        src = at_x(nx - d)
        remote(wq_part(src), wq.at[src], xw_s.at[d], xw_r.at[d], {"x": src}).wait_recv()
    relayed(0, opposite, left_x).wait_recv()
    relayed(1, opposite, right_x).wait_recv()

    @pl.when(x != 0)
    def _():
        remote(kvs.at[0], kvw.at[0], kv_s.at[0], kv_r.at[0], {"x": x // 2}).wait_recv()

    @pl.when(x != nx - 1)
    def _():
        remote(kvs.at[0], kvw.at[1], kv_s.at[0], kv_r.at[1], {"x": x // 2}).wait_recv()

    steps = nz // 4
    sides = ((1, r_even, r_odd, re_s, re_r, ro_s, ro_r), (-1, l_even, l_odd, le_s, le_r, lo_s, lo_r))

    def along(side, d):
        return at_z(d if side[0] > 0 else nz - d)

    def odd_copy(side, i, k):
        src = part.at[along(side, 2 * i + 1), k]
        to = {"z": along(side, 1)}
        return remote(src, side[2].at[i, k], side[5].at[i, k], side[6].at[i, k], to)

    def even_copy(side, s, k):
        if s == 0:
            src = part.at[along(side, 2 * steps), k]
        elif s == 1 and side[0] < 0:
            src = side[2].at[steps - 1, k]
        else:
            src = side[1].at[s - 1, k]
        to = {"z": along(side, 2)}
        return remote(src, side[1].at[s, k], side[3].at[s, k], side[4].at[s, k], to)

    def start_piece(k):
        send(even_copy(sides[0], 0, k))
        for side in sides:
            send(odd_copy(side, steps - 1, k))

    for k in range(0, pieces - 1, 2):
        cols = slice(k * HD, (k + 2) * HD)
        total = dot(nrm[:, :kw], wq[0, :, cols])
        for t in range(1, nx):
            total = total + dot(nrm[:, t * kw : (t + 1) * kw], wq[t, :, cols])
        for h in range(2):
            part[:, k + h] = total[:, h * HD : (h + 1) * HD].reshape(nz, per_z, HD)
            start_piece(k + h)
    half = nrm[:, pl.ds(pl.multiple_of(lax.rem(x, 2) * 2 * kw, 2 * kw), 2 * kw)]
    kv_part = dot(half[:, :kw], kvw[0]) + dot(half[:, kw:], kvw[1])
    part[:, pieces - 1] = kv_part.reshape(nz, per_z, HD)
    start_piece(pieces - 1)
    for k in range(pieces):
        for side in sides:
            send(odd_copy(side, steps - 2, k))
    for s in range(1, steps):
        for k in range(pieces):
            for side in sides:
                own_part = part[along(side, 2 * (steps - s)), k]
                odd_copy(side, steps - s, k).wait_recv()
                if s == 1 and side[0] < 0:
                    side[2][steps - 1, k] = side[2][steps - 1, k] + own_part
                else:
                    even_copy(side, s - 1, k).wait_recv()
                    side[1][s - 1, k] = side[1][s - 1, k] + side[2][steps - s, k] + own_part
                send(even_copy(side, s, k))
        if s + 1 < steps:
            for k in range(pieces):
                for side in sides:
                    send(odd_copy(side, steps - s - 2, k))
    for k in range(pieces):
        own = part[z, k]
        for side in sides:
            odd_copy(side, 0, k).wait_recv()
            even_copy(side, steps - 1, k).wait_recv()
            own = own + side[1][steps - 1, k] + side[2][0, k]
        for t in range(nx):
            xs[t, k] = own[t * slots : (t + 1) * slots]
        for d in (2, 1, nx - 1):
            to = at_x(d)
            send(remote(xs.at[to, k], xin.at[x, k], xe_s.at[d, k], xe_r.at[d, k], {"x": to}))
    xin[x] = xs[x]

    tab_in.wait()
    lengths = [lens[asg[w_own * slots + j]] for j in range(slots)]
    angles = jnp.concatenate([tab[pl.ds(lengths[j], 1), :] for j in range(slots)], axis=0)
    turned = pltpu.roll(angles, HD // 2, 1)
    lane = lax.broadcasted_iota(jnp.int32, (slots, HD), 1)
    cosine = jnp.where(lane < HD // 2, angles, turned)
    sine = jnp.where(lane < HD // 2, -turned, angles)

    def rotate(v):
        return (v * cosine + pltpu.roll(v, HD // 2, 1) * sine).astype(BF16).astype(F32)

    for i in range(pieces):
        for d in range(1, nx):
            src = at_x(nx - d)
            remote(xs.at[0, i], xin.at[src, i], xe_s.at[d, i], xe_r.at[d, i], {"x": src}).wait_recv()
        for k in range(nx if i < heads_x else 0):
            turned_query = rotate(xin[k, i])
            for j in range(slots):
                q_ref[j, k * heads_x + i : k * heads_x + i + 1, :] = turned_query[j : j + 1]
    keys_new = rotate(xin[0, pieces - 1] + xin[1, pieces - 1])
    values_new = (xin[2, pieces - 1] + xin[3, pieces - 1]).astype(BF16).astype(F32)

    scale = 1.0 / math.sqrt(HD)
    position = lax.broadcasted_iota(jnp.int32, (heads, most), 1)
    for j in range(slots):
        query = q_ref[j]
        own_score = jnp.sum(query * keys_new[j : j + 1], axis=1, keepdims=True) * scale
        scores = dot_t(query.astype(BF16), kc[j]) * scale
        scores = jnp.where(position < lengths[j], scores, -jnp.inf)
        top = jnp.maximum(jnp.max(scores, axis=1, keepdims=True), own_score)
        weights = jnp.exp(scores - top)
        own_weight = jnp.exp(own_score - top)
        totals = jnp.sum(weights, axis=1, keepdims=True) + own_weight
        probs = (weights / totals).astype(BF16)
        own_prob = (own_weight / totals).astype(BF16).astype(F32)
        attended = dot(probs, vc[j]) + own_prob * values_new[j : j + 1]
        for h in range(heads):
            ab[j : j + 1, h * HD : (h + 1) * HD] = attended[h : h + 1]
    ag[w_own] = ab[...].astype(BF16)

    def z_copy(d, block, to):
        return remote(ag.at[block], ag.at[block], az_s.at[d], az_r.at[d], {"z": to})

    def x_copy(d, e, block, to):
        return remote(ag.at[block], ag.at[block], ax_s.at[d, e], ax_r.at[d, e], {"x": to})

    def block_of(e, d):
        return at_x(nx - e) * nz + at_z(nz - d)

    def along_x(d, hops):
        for e in hops:
            send(x_copy(d, e, block_of(0, d), at_x(e)))

    for k in range(reach, 0, -1):
        send(z_copy(k, w_own, at_z(k)))
        send(z_copy(nz - k, w_own, at_z(nz - k)))
    order = [0] + by_distance(nz)
    near = [d for d in order if min(d, nz - d) <= reach]
    far = [d for d in order if min(d, nz - d) > reach]
    along_x(0, (1, nx - 1))
    for d in (reach, nz - reach):
        z_copy(d, block_of(0, d), z).wait_recv()
        if d == reach:
            for k in range(reach, 0, -1):
                send(z_copy(reach + k, block_of(0, d), at_z(k)))
        else:
            for k in range(reach - 1, 0, -1):
                send(z_copy(nz - reach - k, block_of(0, d), at_z(nz - k)))
    for d in near[1:]:
        if d not in (reach, nz - reach):
            z_copy(d, block_of(0, d), z).wait_recv()
        along_x(d, (1, nx - 1))
    for d in near:
        e = 1 if d % 2 == 0 else nx - 1
        x_copy(d, e, block_of(e, d), x).wait_recv()
        send(x_copy(d, 2, block_of(e, d), at_x(e)))
    for d in far:
        z_copy(d, block_of(0, d), z).wait_recv()
        along_x(d, (2, 1, nx - 1))
    wo_in.wait()
    for d in order:
        passed = 1 if d % 2 == 0 else nx - 1
        for e in range(1, nx):
            if d in far or e != passed:
                x_copy(d, e, block_of(e, d), x).wait_recv()

    group = 16 // slots
    for g in range(rows // 16):
        blocks = [ag[g * group + i].astype(F32) for i in range(group)]
        att[g * 16 : (g + 1) * 16, :] = jnp.concatenate(blocks, axis=0).astype(BF16)
    tile = 512
    update = jnp.zeros((rows, wo.shape[1]), F32)
    for k in range(att.shape[1] // tile):
        cols = slice(k * tile, (k + 1) * tile)
        update = update + dot(att[:, cols], wo[cols, :])
    rounded = update.astype(BF16)
    rest = (update - rounded.astype(F32)).astype(BF16)
    picked = dot(pr[...], rounded)
    nst[...] = picked.astype(BF16).reshape(nn, rows_n, wo.shape[1])
    for d in far_first:
        send(remote(nst.at[at_n(d)], nin.at[d], no_s.at[d], no_r.at[d], {"narrow": at_n(d)}))
    own_pick = pr[pl.ds(pl.multiple_of(n * rows_n, rows_n), rows_n), :]
    result = nst[n].astype(F32) + dot(own_pick, rest)
    for d in range(1, nn):
        src = at_n(nn - d)
        remote(nst.at[0], nin.at[d], no_s.at[d], no_r.at[d], {"narrow": src}).wait_recv()
        result = result + nin[d].astype(F32)
    out_ref[...] = (nres[n, x].astype(F32) + result).astype(BF16)

    for copy in sends:
        copy.wait_send()

    @pl.when(x != 0)
    def _():
        k_copy.wait_send()

    @pl.when(x != nx - 1)
    def _():
        v_copy.wait_send()


def per_device(nx, nz, nn, table, residual, norm_gain, w_query, w_keyval, w_out, cache_rows, lengths, assignment):
    slots, most, _, channels = cache_rows.shape
    kw, query_cols = w_query.shape
    rows_n = residual.shape[0]
    rows = rows_n * nn
    qcols = query_cols // nx
    pieces = qcols // HD + 1
    heads = query_cols // HD
    steps = nz // 4
    width = kw * nx * nz
    anywhere = pl.BlockSpec(memory_space=pl.ANY)
    vmem = pl.BlockSpec(memory_space=pltpu.VMEM)
    smem = pl.BlockSpec(memory_space=pltpu.SMEM)
    dma = pltpu.SemaphoreType.DMA
    scratch = [
        pltpu.VMEM((nn, nx, rows_n, kw), BF16),
        pltpu.VMEM((nx, 1, kw), F32),
        pltpu.VMEM((nx, kw, qcols), BF16),
        pltpu.VMEM((2 * kw, HD), BF16),
        pltpu.VMEM((2, kw, HD), BF16),
        pltpu.VMEM((2, kw, HD), BF16),
        pltpu.VMEM(w_out.shape, BF16),
        pltpu.VMEM((slots * most * 2, HD), BF16),
        pltpu.VMEM((slots, most, HD), BF16),
        pltpu.VMEM((slots, most, HD), BF16),
        pltpu.VMEM(table.shape, F32),
        pltpu.VMEM((kw,), BF16),
        pltpu.VMEM((nz, 1, rows), F32),
        pltpu.VMEM((nn, 1, rows), F32),
        pltpu.VMEM((rows, rows), BF16),
        pltpu.VMEM((rows, rows), BF16),
        pltpu.VMEM((rows, nx * kw), BF16),
        pltpu.VMEM((rows, nx * kw), BF16),
        pltpu.VMEM((nz, pieces, nx * slots, HD), F32),
        pltpu.VMEM((steps, pieces, nx * slots, HD), F32),
        pltpu.VMEM((steps, pieces, nx * slots, HD), F32),
        pltpu.VMEM((steps, pieces, nx * slots, HD), F32),
        pltpu.VMEM((steps, pieces, nx * slots, HD), F32),
        pltpu.VMEM((2, kw // 2, qcols), BF16),
        pltpu.VMEM((nx, pieces, slots, HD), F32),
        pltpu.VMEM((nx, pieces, slots, HD), F32),
        pltpu.VMEM((slots, heads, HD), F32),
        pltpu.VMEM((slots, query_cols), F32),
        pltpu.VMEM((nx * nz, slots, query_cols), BF16),
        pltpu.VMEM((rows, query_cols), BF16),
        pltpu.VMEM((nn, rows_n, w_out.shape[1]), BF16),
        pltpu.VMEM((nn, rows_n, w_out.shape[1]), BF16),
        dma((7,)),
        dma((nx,)), dma((nx,)), dma((nx,)), dma((nx,)), dma((nx,)), dma((nx,)),
        dma((2,)), dma((2,)),
        dma((7,)), dma((7,)),
        dma((nz,)), dma((nz,)),
        dma((nn,)), dma((nn,)),
        *[dma((steps, pieces))] * 8,
        dma((2,)), dma((2,)), dma((2,)), dma((2,)),
        dma((nx, pieces)), dma((nx, pieces)),
        dma((nz,)), dma((nz,)), dma((nz, nx)), dma((nz, nx)),
        dma((nn,)), dma((nn,)),
    ]
    return pl.pallas_call(
        functools.partial(kernel, nx, nz, nn, width),
        out_shape=jax.ShapeDtypeStruct(residual.shape, BF16),
        in_specs=[smem, smem, anywhere, anywhere, vmem] + [anywhere] * 5,
        out_specs=vmem,
        scratch_shapes=scratch,
        compiler_params=pltpu.CompilerParams(
            collective_id=0, has_side_effects=True, vmem_limit_bytes=60 * 1024 * 1024
        ),
        name="decode_block",
    )(
        lengths,
        assignment,
        residual,
        norm_gain,
        assignment.reshape(1, -1),
        w_query,
        w_keyval.reshape(2 * kw, channels),
        w_out,
        cache_rows.reshape(slots * most * 2, channels),
        table,
    )


def solution(mesh):
    nx, nn = 4, mesh.shape["narrow"]
    nz = mesh.shape["wide"] // nx
    torus = Mesh(mesh.devices.reshape(nx, nz, nn), ("x", "z", "narrow"))
    wide = ("x", "z")

    def run(residual, norm_gain, w_query, w_keyval, w_out, cache_rows, lengths, assignment):
        table = jnp.asarray(rotation_table(cache_rows.shape[1]))
        body = jax.shard_map(
            lambda table, *args: per_device(nx, nz, nn, table, *args),
            mesh=torus,
            in_specs=(
                P(),
                P("narrow", wide),
                P(wide),
                P(wide, "narrow"),
                P(wide, None, "narrow"),
                P("narrow", wide),
                P(wide, None, None, "narrow"),
                P(),
                P(),
            ),
            out_specs=P("narrow", wide),
            check_vma=False,
        )
        return body(table, residual, norm_gain, w_query, w_keyval, w_out, cache_rows, lengths, assignment)

    return run
```
